512 devices in a mesh: ctx: 8 (over y), dp: 64 (over x, z, core).
Axes of the slice: x: 4, y: 8, z: 8, core: 2. Of those that a mesh axis runs over, the one named last changes fastest.
Arguments:
- queries: bfloat16 [64, 1024, 1024], P('dp', 'ctx'), may hold values from -20 to 20
- keys: bfloat16 [64, 1024, 1024], P('dp', 'ctx'), may hold values from -4 to 4
- values: bfloat16 [64, 1024, 1024], P('dp', 'ctx'), may hold values from -16 to 16
- d_mixed: bfloat16 [64, 1024, 1024], P('dp', 'ctx'), may hold values from -6 to 6
- series_ids: int32 [64, 1024], P('dp', 'ctx'), may hold values from 0 to 15, never falling along the last dimension, each value on 1 to 576 neighbouring positions
- variate_ids: int32 [64, 1024], P('dp', 'ctx'), may hold values from 0 to 3
- variate_bias: float32 [2, 16], replicated, may hold values from -4 to 4
- w_out: bfloat16 [1024, 1024], P('dp'), may hold values from -0.1875 to 0.1875
Outputs:
- mixed: bfloat16 [64, 1024, 1024], P('dp', 'ctx')
- q_grad: bfloat16 [64, 1024, 1024], P('dp', 'ctx')
- k_grad: bfloat16 [64, 1024, 1024], P('dp', 'ctx')
- v_grad: bfloat16 [64, 1024, 1024], P('dp', 'ctx')
- w_grad: float32 [1024, 1024], P('dp')
- bias_grad: float32 [2, 16], replicated
The draws below stay inside these ranges and needn't reach their ends.
Inputs may be any that keep to these rules, and one draw needn't show every extreme that they name: `series_ids`: within a packed row series numbers never fall; each series spans 1 to 576 consecutive tokens and some series spans exactly 576.
All inputs are finite; a program needn't handle non-finite values.
Results may differ from the reference program's by a relative error of at most 0.015.
Values may be sent and summed in bfloat16 or wider, within the bound.
A program may use at most 128 MiB of HBM per device.

```python
import math
import jax
import jax.numpy as jnp
import numpy as np
from jax import lax

D = 1024
HEADS = 16
HEAD_DIM = 64
VARIATES = 4
BATCH = 64
ROW = 1024
SERIES = 16
MOST = 576


def pair_draw(key):
    base = jax.random.fold_in(key, 911)
    key_query, key_key = jax.random.split(base)
    shape = (BATCH, ROW, D)
    keys_drawn = jnp.clip(jax.random.normal(key_key, shape, jnp.float32), -4.0, 4.0)
    queries_drawn = jnp.clip(jax.random.normal(key_query, shape, jnp.float32), -4.0, 4.0)
    return (queries_drawn, keys_drawn)


def draw_queries(key, part):
    return pair_draw(key)[0].astype(jnp.bfloat16)


def draw_keys(key, part):
    return pair_draw(key)[1].astype(jnp.bfloat16)


def with_ends(entries, rng, smallest, high):
    index_at = [jax.random.randint(jax.random.fold_in(rng, axis), (), 0, length) for axis, length in enumerate(entries.shape)]
    widest = entries.shape.index(max(entries.shape))
    next_to = index_at[:widest] + [(index_at[widest] + 1) % entries.shape[widest]] + index_at[widest + 1:]
    return entries.at[tuple(index_at)].set(smallest).at[tuple(next_to)].set(high)


def spiked(values, key, source, target, blocks, factor):
    owner, partner = [(jnp.arange(values.shape[dim]) // (values.shape[dim] // blocks)).reshape([-1 if axis == dim else 1 for axis in range(values.ndim)]) for dim in (source, target)]
    chosen = jax.random.permutation(key, blocks)[partner]
    strong = (owner == chosen) | (owner == (partner + blocks // 2) % blocks)
    return jnp.where(strong, factor * values, values)


def block_levels(rng, shape, shards, smallest, high):
    level, own = 1.0, jax.random.fold_in(rng, 6)
    for position, shards_of in shards:
        heights = jnp.exp(jax.random.uniform(jax.random.fold_in(own, position), (shards_of,), jnp.float32, smallest / len(shards), high / len(shards)))
        level = level * jnp.repeat(heights, shape[position] // shards_of).reshape([-1 if axis == position else 1 for axis in range(len(shape))])
    return level


def profile(count, total, reach, lean):
    weights = [(1 << 20) // math.isqrt(standing ** lean) + 1 for standing in range(2, count + 1)]
    spare, counts = total - reach - (count - 1), [1] * (count - 1)
    while spare > 0:
        free = [i for i in range(count - 1) if counts[i] < reach]
        mass, left = sum([weights[i] for i in free]), spare
        for i in free:
            addition = min(reach - counts[i], max(1, left * weights[i] // mass), spare)
            counts[i] = counts[i] + addition
            spare = spare - addition
    return np.array([reach] + counts)


def uneven(rng, count, total, limit, skew):
    if count == 2:
        one = jax.random.randint(rng, (), max(1, total - limit), min(limit, total - 1) + 1)
        return jnp.stack([one, total - one])
    lengths = jnp.asarray(profile(count, total, limit, skew), jnp.int32)
    twos = (count - 1) // 2
    source_of, sink = lengths[1:1 + 2 * twos:2], lengths[2:2 + 2 * twos:2]
    room = jnp.minimum(source_of - 1, limit - sink)
    moved = jax.random.randint(jax.random.fold_in(rng, 1), (twos,), 0, 1 << 20) % (room + 1)
    lengths = lengths.at[1:1 + 2 * twos:2].set(source_of - moved).at[2:2 + 2 * twos:2].set(sink + moved)
    return lengths[jax.random.permutation(jax.random.fold_in(rng, 2), count)]


def bell_draw(key, shape, deviation, reach, shards=(), dtype=jnp.bfloat16):
    values = deviation * jax.random.normal(key, shape, jnp.float32)
    if shards:
        values = values * block_levels(key, shape, shards, -0.22, 0.18)
    return jnp.clip(values, -reach, reach).astype(dtype)


def gaussian_with(key, dims, deviation, bound, pieces, heavy, held_as=jnp.bfloat16):
    values = deviation * jax.random.normal(key, dims, jnp.float32)
    if pieces:
        values = values * block_levels(key, dims, pieces, -0.22, 0.18)
    return jnp.clip(spiked(values, jax.random.fold_in(key, 3), *heavy), -bound, bound).astype(held_as)


def setup_inputs(seed: int = 0) -> dict:
    splits = jax.random.split(jax.random.key(seed), 9)
    queries = draw_queries(jax.random.fold_in(splits[8], 71), 0)
    keys = draw_keys(jax.random.fold_in(splits[8], 71), 0)
    values = gaussian_with(splits[2], (BATCH, ROW, D), 1.0, 16.0, ((0, 64), (1, 8)), (0, 2, 64, 4.0))
    d_mixed = bell_draw(splits[3], (BATCH, ROW, D), 1.0, 6.0, ((0, 64), (1, 8)))
    series_ids = jax.vmap(lambda own: jnp.searchsorted(jnp.cumsum(uneven(own, SERIES, ROW, MOST, 2)), jnp.arange(ROW), side="right"))(jax.random.split(splits[4], BATCH)).reshape((BATCH, ROW)).astype(jnp.int32)
    variate_ids = with_ends(jax.random.randint(splits[5], (BATCH, ROW), 0, VARIATES), jax.random.fold_in(splits[5], 1), 0, VARIATES - 1).astype(jnp.int32)
    variate_bias = bell_draw(splits[6], (2, HEADS), 1.0, 4.0, (), jnp.float32)
    w_out = bell_draw(splits[7], (D, D), D ** -0.5, 0.1875, ((0, 64),))
    return dict(queries=queries, keys=keys, values=values, d_mixed=d_mixed, series_ids=series_ids, variate_ids=variate_ids, variate_bias=variate_bias, w_out=w_out)


NEG = -1e30


def barrier_round(values):
    return lax.optimization_barrier(values.astype(jnp.bfloat16)).astype(jnp.float32)


def reference(queries, keys, values, d_mixed, series_ids, variate_ids, variate_bias, w_out):
    scale = HEAD_DIM ** -0.5

    def one_row(carry, row):
        w_sum, b_sum = carry
        query, key_rows, value_rows, upstream, series, variate = row
        qf = query.astype(jnp.float32).reshape(ROW, HEADS, HEAD_DIM)
        kf = key_rows.astype(jnp.float32).reshape(ROW, HEADS, HEAD_DIM)
        vf = value_rows.astype(jnp.float32).reshape(ROW, HEADS, HEAD_DIM)
        allowed = (series[:, None] == series[None, :])[None]
        same = (variate[:, None] == variate[None, :])[None]
        addend = jnp.where(same, variate_bias[0][:, None, None], variate_bias[1][:, None, None])
        scores = jnp.einsum("qhd,khd->hqk", qf, kf) * scale + addend
        scores = jnp.where(allowed, scores, NEG)
        top = jnp.max(scores, axis=2, keepdims=True)
        total = jnp.sum(jnp.where(allowed, jnp.exp(scores - top), 0.0), axis=2, keepdims=True)
        lse = top + jnp.log(total)
        probs = jnp.where(allowed, jnp.exp(scores - lse), 0.0)
        weights = barrier_round(probs)
        context = jnp.einsum("hqk,khd->qhd", weights, vf)
        context_bf = context.reshape(ROW, D).astype(jnp.bfloat16)
        mixed = jnp.dot(context_bf, w_out, preferred_element_type=jnp.float32).astype(jnp.bfloat16)
        d_context = jnp.dot(upstream, w_out.T, preferred_element_type=jnp.float32).astype(jnp.bfloat16)
        w_sum = w_sum + jnp.dot(context_bf.T, upstream, preferred_element_type=jnp.float32)
        df = d_context.astype(jnp.float32).reshape(ROW, HEADS, HEAD_DIM)
        delta = jnp.einsum("qhd,qhd->hq", df, context)
        dprob = jnp.einsum("qhd,khd->hqk", df, vf)
        dscore = probs * (dprob - delta[:, :, None])
        dround = barrier_round(dscore)
        q_grad = (jnp.einsum("hqk,khd->qhd", dround, kf) * scale).reshape(ROW, D).astype(jnp.bfloat16)
        k_grad = (jnp.einsum("hqk,qhd->khd", dround, qf) * scale).reshape(ROW, D).astype(jnp.bfloat16)
        v_grad = jnp.einsum("hqk,qhd->khd", weights, df).reshape(ROW, D).astype(jnp.bfloat16)
        b_row = jnp.stack([jnp.sum(jnp.where(same, dscore, 0.0), axis=(1, 2)),
                           jnp.sum(jnp.where(same, 0.0, dscore), axis=(1, 2))])
        return (w_sum, b_sum + b_row), (mixed, q_grad, k_grad, v_grad)

    start = (jnp.zeros((D, D), jnp.float32), jnp.zeros((2, HEADS), jnp.float32))
    (w_grad, bias_grad), (mixed, q_grad, k_grad, v_grad) = lax.scan(
        one_row, start, (queries, keys, values, d_mixed, series_ids, variate_ids))
    return mixed, q_grad, k_grad, v_grad, w_grad, bias_grad
```

```python
import functools

import jax
import jax.numpy as jnp
from jax import lax
from jax.experimental import pallas as pl
from jax.experimental.pallas import tpu as pltpu
from jax.sharding import Mesh
from jax.sharding import PartitionSpec as P

HEADS = 16
HEAD_DIM = 64
NY, NX, NZ, NC = 8, 4, 8, 2
TOK = 128
ROW = 1024
D = 1024
DP = ("x", "z", "core")
MESH = pl.DeviceIdType.MESH
F32 = jnp.float32
BF16 = jnp.bfloat16
ORDER = (1, 7, 2, 6, 3, 5, 4)
MASK = 2048.0
BQ = 128


def remote(src, dst, ssem, rsem, **where):
    return pltpu.make_async_remote_copy(
        src_ref=src, dst_ref=dst, send_sem=ssem, recv_sem=rsem,
        device_id=where, device_id_type=MESH,
    )


def meet(peers):
    sem = pltpu.get_barrier_semaphore()
    for peer in peers:
        pl.semaphore_signal(sem, inc=1, device_id=peer, device_id_type=MESH)
    pl.semaphore_wait(sem, len(peers))


def others(axis, n):
    me = lax.axis_index(axis)
    return [{axis: lax.rem(me + d, n)} for d in range(1, n)]


def span(i, n=128):
    return pl.ds(pl.multiple_of(i * n, n), n)


def spread(src, dst, ssem, rsem, lsem):
    me = lax.axis_index("ctx")
    copies = []
    for d in ORDER:
        to = lax.rem(me + d, NY)
        c = remote(src.at[:, span(to)], dst.at[span(me), :], ssem.at[d], rsem.at[d], ctx=to)
        c.start()
        copies.append(c)
    c = pltpu.make_async_copy(src.at[:, span(me)], dst.at[span(me), :], lsem)
    c.start()
    copies.append(c)
    return copies


def unspread(src, dst, ssem, rsem, lsem):
    me = lax.axis_index("ctx")
    copies = []
    for d in ORDER:
        to = lax.rem(me + d, NY)
        c = remote(src.at[span(to), :], dst.at[:, span(me)], ssem.at[d], rsem.at[d], ctx=to)
        c.start()
        copies.append(c)
    c = pltpu.make_async_copy(src.at[span(me), :], dst.at[:, span(me)], lsem)
    c.start()
    copies.append(c)
    return copies


def gather_kernel(q, k, v, dm, ser, var, w,
                  qh, kh, vh, dh, ser_o, var_o, wf,
                  dctx, a_s, a_r, a_l, i_s, i_r, i_l, x_s, x_r, z_s, z_r, c_s, c_r, w_l):
    y, x, z, c = (lax.axis_index(a) for a in ("ctx", "x", "z", "core"))
    sib = 1 - c
    up, down = lax.rem(z + 1, NZ), lax.rem(z + NZ - 1, NZ)
    meet(others("ctx", NY) + others("x", NX) + [{"z": up}, {"z": down}, {"core": sib}])
    own = pltpu.make_async_copy(w, wf.at[x, z, c], w_l)
    own.start()
    todo = []
    for d in range(1, NX):
        to = lax.rem(x + d, NX)
        cp = remote(w, wf.at[x, z, c], x_s.at[d], x_r.at[d], x=to)
        cp.start()
        todo.append(cp)
    x_copies = todo[:]
    todo = []
    for n, (src, dst) in enumerate(((ser, ser_o), (var, var_o))):
        for d in ORDER:
            to = lax.rem(y + d, NY)
            cp = remote(src, dst.at[:, span(y)], i_s.at[n, d], i_r.at[n, d], ctx=to)
            cp.start()
            todo.append(cp)
        cp = pltpu.make_async_copy(src, dst.at[:, span(y)], i_l.at[n])
        cp.start()
        todo.append(cp)
    for n, (src, dst) in enumerate(((q, qh), (k, kh), (v, vh))):
        todo += spread(src, dst, a_s.at[n], a_r.at[n], a_l.at[n])

    own.wait()
    arrived = {}
    sub = [lax.rem(x + NX - j, NX) for j in range(NX)]

    def block(zz, j):
        return wf.at[sub[j], zz, c]

    def to_sibling(zz, j, n):
        cp = remote(block(zz, j), block(zz, j), c_s.at[n, j], c_r.at[n, j], core=sib)
        cp.start()
        todo.append(cp)

    for s in range(4):
        zr, zl = lax.rem(z + NZ - s, NZ), lax.rem(z + s, NZ)
        for j in range(NX):
            if s == 0:
                if j > 0:
                    x_copies[j - 1].wait()
            else:
                arrived[(0, s - 1, j)].wait()
            cp = remote(block(zr, j), block(zr, j), z_s.at[0, s, j], z_r.at[0, s, j], z=up)
            cp.start()
            arrived[(0, s, j)] = cp
            if s < 3:
                if s > 0:
                    arrived[(1, s - 1, j)].wait()
                cp = remote(block(zl, j), block(zl, j), z_s.at[1, s, j], z_r.at[1, s, j], z=down)
                cp.start()
                arrived[(1, s, j)] = cp
            to_sibling(zr, j, s)
            if 0 < s < 3:
                to_sibling(zl, j, 4 + s)
    zr, zl = lax.rem(z + NZ - 4, NZ), lax.rem(z + 3, NZ)
    for j in range(NX):
        arrived[(1, 2, j)].wait()
        to_sibling(zl, j, 7)
        arrived[(0, 3, j)].wait()
        to_sibling(zr, j, 4)
    for cp in todo[-8 * NX:]:
        cp.wait()
    todo = todo[:-8 * NX]

    for xi in range(NX):
        rows = wf[xi].reshape(256, D)
        got = lax.dot_general(dm[...], rows, (((1,), (1,)), ((), ())), preferred_element_type=F32)
        dctx[:, 256 * xi:256 * (xi + 1)] = got.astype(BF16)
    todo += spread(dctx, dh, a_s.at[3], a_r.at[3], a_l.at[3])
    for cp in todo:
        cp.wait()


def attention_kernel(qh, kh, vh, dh, ser, var, bias,
                     ctx, dq, dk, dv, bt,
                     base_s, qa_s, ka_s, va_s, qt_s, dkt, dvt):
    me = lax.axis_index("ctx")
    feat = lax.broadcasted_iota(jnp.int32, (128, ROW), 0) % 64
    held = jnp.where(feat < 16, ser[...], var[...])
    want = jnp.where(feat < 16, feat, jnp.where(feat < 28, feat % 4, -1))
    base_t = jnp.where(held == want, 1.0, 0.0)
    base = base_t.T
    base_s[...] = base
    lane = lax.broadcasted_iota(jnp.int32, (1, 128), 1)
    within = lane % 64
    qt_s[...] = (qh[...].astype(F32) * 0.125).T.astype(BF16)
    dkt[...] = jnp.zeros_like(dkt)
    dvt[...] = jnp.zeros_like(dvt)
    for h in range(2):
        mine = (lane // 64) == h
        gap = bias[0, 2 * me + h] - bias[1, 2 * me + h]
        gap = jnp.full((1, 128), gap, F32)
        hi = gap.astype(BF16).astype(F32)
        mid = (gap - hi).astype(BF16).astype(F32)
        low = gap - hi - mid
        coef = jnp.where(within < 16, MASK, jnp.where(within < 20, hi, jnp.where(within < 24, mid, low)))
        qa_s[h] = jnp.where(mine, qh[...].astype(F32) * 0.125, base * coef).astype(BF16)
        ka_s[h] = jnp.where(mine, kh[...].astype(F32), base).astype(BF16)
        va_s[h] = jnp.where(mine, vh[...].astype(F32), 1.0).astype(BF16)

    def step(i, carry):
        rows = span(i, BQ)
        d_blk = dh[rows, :].astype(F32)
        o_blk = base_s[rows, :]
        merged = []
        sums = []
        for h in range(2):
            mine = (lane // 64) == h
            s = lax.dot_general(qa_s[h, rows, :], ka_s[h], (((1,), (1,)), ((), ())),
                                preferred_element_type=F32)
            top = jnp.max(s, axis=1, keepdims=True)
            e = jnp.exp(s - top)
            eb = e.astype(BF16)
            un = jnp.dot(eb, va_s[h], preferred_element_type=F32)
            inv = 1.0 / pltpu.roll(un, 64, 1)
            c = un * inv
            dn = (d_blk * inv).astype(BF16)
            dnf = dn.astype(F32)
            delta = jnp.sum(jnp.where(mine, dnf * c, 0.0), axis=1, keepdims=True)
            hi = delta.astype(BF16).astype(F32)
            mid = (delta - hi).astype(BF16).astype(F32)
            low = delta - hi - mid
            da = jnp.where(within == 0, -hi, jnp.where(within == 1, -mid, jnp.where(within == 2, -low, 0.0)))
            da = jnp.where(mine, dnf, da).astype(BF16)
            t = lax.dot_general(da, va_s[h], (((1,), (1,)), ((), ())), preferred_element_type=F32)
            ds = (e * t).astype(BF16)
            g = jnp.dot(ds, ka_s[h], preferred_element_type=F32)
            half = slice(64 * h, 64 * (h + 1))
            dn_t = jnp.where(mine, dnf, 0.0).T[half].astype(BF16)
            dvt[half, :] += jnp.dot(dn_t, eb, preferred_element_type=F32)
            q_t = qt_s[half, rows]
            dkt[half, :] += jnp.dot(q_t, ds, preferred_element_type=F32)
            wanted = jnp.logical_not(mine) & (within >= 16) & (within < 20)
            u = jnp.where(wanted, g, 0.0)
            sums.append(jnp.sum(u * o_blk, axis=0, keepdims=True))
            sums.append(jnp.sum(u * (1.0 - o_blk), axis=0, keepdims=True))
            merged.append((c, g * 0.125))
        ctx[rows, :] = jnp.where(lane < 64, merged[0][0], merged[1][0]).astype(BF16)
        dq[rows, :] = jnp.where(lane < 64, merged[0][1], merged[1][1]).astype(BF16)
        return tuple(a + b for a, b in zip(carry, sums))

    zero = jnp.zeros((1, 128), F32)
    s0, f0, s1, f1 = lax.fori_loop(0, ROW // BQ, step, (zero,) * 4)
    total = [jnp.sum(a, axis=1, keepdims=True) for a in (s0, f0, s1, f1)]
    row = lax.broadcasted_iota(jnp.int32, (8, 128), 0)
    col = lax.broadcasted_iota(jnp.int32, (8, 128), 1) - 2 * me
    tile = jnp.zeros((8, 128), F32)
    for h in range(2):
        for r in range(2):
            tile = jnp.where((row == r) & (col == h), total[2 * h + r], tile)
    bt[...] = tile
    for b in range(8):
        cols = slice(128 * b, 128 * (b + 1))
        dk[cols, :] = dkt[:, cols].T.astype(BF16)
        dv[cols, :] = dvt[:, cols].T.astype(BF16)


def return_kernel(ctxh, dqh, dkh, dvh, bt, dm, wf,
                  mixed, dq, dk, dv, wg, bg,
                  ctx, g, sa, sb_r, sb_l, rr, rl, acc, xs, xr, ys, yr, bs, br,
                  a_s, a_r, a_l, c_s, c_r, z_s, z_r, x_s, x_r, y_s, y_r, b_s, b_r):
    y, x, z, c = (lax.axis_index(a) for a in ("ctx", "x", "z", "core"))
    sib = 1 - c
    up, down = lax.rem(z + 1, NZ), lax.rem(z + NZ - 1, NZ)
    meet(others("ctx", NY) + others("x", NX) + others("z", NZ) + [{"core": sib}])
    first = unspread(ctxh, ctx, a_s.at[0], a_r.at[0], a_l.at[0])
    todo = []
    for n, (src, dst) in enumerate(((dvh, dv), (dkh, dk), (dqh, dq))):
        todo += unspread(src, dst, a_s.at[n + 1], a_r.at[n + 1], a_l.at[n + 1])
    bsib = remote(bt, br.at[0], b_s.at[0], b_r.at[0], core=sib)
    bsib.start()
    for cp in first:
        cp.wait()
    for xi in range(NX):
        part = ctx[:, 256 * xi:256 * (xi + 1)].astype(F32).T.astype(BF16)
        got = jnp.dot(part, dm[...], preferred_element_type=F32)
        g[xi] = got.astype(BF16).reshape(8, 2, 16, D)

    sibs = {}
    for off in (4, 5, 3, 6, 2, 7, 1, 0):
        zt = lax.rem(z + off, NZ)
        cp = remote(g.at[:, zt, sib], sa.at[:, zt], c_s.at[off], c_r.at[off], core=sib)
        cp.start()
        sibs[off] = cp

    bsib.wait()
    bs[0] = bt[...] + br[0]
    bz = []
    for d in range(1, NZ):
        cp = remote(bs.at[0], br.at[d], b_s.at[d], b_r.at[d], z=lax.rem(z + d, NZ))
        cp.start()
        bz.append(cp)

    def part_sum(off):
        zt = lax.rem(z + off, NZ)
        sibs[off].wait()
        return g[:, zt, c].astype(F32) + sa[:, zt].astype(F32)

    r_cp, l_cp = [], []
    for s in range(4):
        val = part_sum(4 - s)
        if s > 0:
            r_cp[s - 1].wait()
            val = val + rr[s - 1].astype(F32)
        sb_r[s] = val.astype(BF16)
        cp = remote(sb_r.at[s], rr.at[s], z_s.at[0, s], z_r.at[0, s], z=up)
        cp.start()
        r_cp.append(cp)
        if s < 3:
            val = part_sum(5 + s)
            if s > 0:
                l_cp[s - 1].wait()
                val = val + rl[s - 1].astype(F32)
            sb_l[s] = val.astype(BF16)
            cp = remote(sb_l.at[s], rl.at[s], z_s.at[1, s], z_r.at[1, s], z=down)
            cp.start()
            l_cp.append(cp)
        got = jnp.dot(ctx[...], wf[...].reshape(D, D)[:, 256 * s:256 * (s + 1)], preferred_element_type=F32)
        mixed[:, 256 * s:256 * (s + 1)] = got.astype(BF16)
    own = part_sum(0)
    for cp in bz:
        cp.wait()
    tile = bs[0]
    for d in range(1, NZ):
        tile = tile + br[d]
    bs[1] = tile
    bx = []
    for d in range(1, NX):
        cp = remote(bs.at[1], br.at[7 + d], b_s.at[7 + d], b_r.at[7 + d], x=lax.rem(x + d, NX))
        cp.start()
        bx.append(cp)
    l_cp[2].wait()
    r_cp[3].wait()
    own = own + rl[2].astype(F32) + rr[3].astype(F32)
    acc[...] = own
    xs[...] = own.astype(BF16)
    xcp = []
    for d in range(1, NX):
        to = lax.rem(x + d, NX)
        cp = remote(xs.at[to], xr.at[d], x_s.at[d], x_r.at[d], x=to)
        cp.start()
        xcp.append(cp)
    for cp in bx:
        cp.wait()
    bs[2] = bs[1] + br[8] + br[9] + br[10]
    by = []
    for d in range(1, NY):
        cp = remote(bs.at[2], br.at[10 + d], b_s.at[10 + d], b_r.at[10 + d], ctx=lax.rem(y + d, NY))
        cp.start()
        by.append(cp)
    for cp in xcp:
        cp.wait()
    ys[...] = acc[x] + xr[1].astype(F32) + xr[2].astype(F32) + xr[3].astype(F32)
    ycp = []
    for d in ORDER:
        to = lax.rem(y + d, NY)
        cp = remote(ys.at[:, span(to)], yr.at[d], y_s.at[0, d], y_r.at[0, d], ctx=to)
        cp.start()
        ycp.append(cp)
    for cp in by:
        cp.wait()
    tile = bs[2]
    for d in range(1, NY):
        tile = tile + br[10 + d]
    bg[...] = tile
    for cp in ycp:
        cp.wait()
    piece = ys[:, span(y)]
    for d in range(1, NY):
        piece = piece + yr[d]
    yr[0] = piece
    wg[:, span(y)] = piece
    last = []
    for d in ORDER:
        to = lax.rem(y + d, NY)
        cp = remote(yr.at[0], wg.at[:, span(y)], y_s.at[1, d], y_r.at[1, d], ctx=to)
        cp.start()
        last.append(cp)
    for cp in last + todo:
        cp.wait()


VM = pl.BlockSpec(memory_space=pltpu.VMEM)
SM = pl.BlockSpec(memory_space=pltpu.SMEM)
DMA = pltpu.SemaphoreType.DMA
LIMIT = 60 * 1024 * 1024


def sds(shape, dtype):
    return jax.ShapeDtypeStruct(shape, dtype)


def on_device(queries, keys, values, d_mixed, series_ids, variate_ids, variate_bias, w_out):
    heads = sds((ROW, 128), BF16)
    qh, kh, vh, dh, ser, var, wf = pl.pallas_call(
        gather_kernel,
        out_shape=[heads] * 4 + [sds((1, ROW), jnp.int32)] * 2 + [sds((NX, NZ, NC, 16, D), BF16)],
        in_specs=[VM] * 7,
        out_specs=[VM] * 7,
        scratch_shapes=[
            pltpu.VMEM((TOK, D), BF16),
            DMA((4, 8)), DMA((4, 8)), DMA((4,)),
            DMA((2, 8)), DMA((2, 8)), DMA((2,)),
            DMA((4,)), DMA((4,)),
            DMA((2, 4, 4)), DMA((2, 4, 4)),
            DMA((8, 4)), DMA((8, 4)), DMA,
        ],
        compiler_params=pltpu.CompilerParams(collective_id=0, has_side_effects=True, vmem_limit_bytes=LIMIT),
        name="gather",
    )(queries[0], keys[0], values[0], d_mixed[0], series_ids, variate_ids, w_out)
    ctxh, dqh, dkh, dvh, bt = pl.pallas_call(
        attention_kernel,
        out_shape=[heads] * 4 + [sds((8, 128), F32)],
        in_specs=[VM] * 6 + [SM],
        out_specs=[VM] * 5,
        scratch_shapes=[
            pltpu.VMEM((ROW, 128), F32),
            pltpu.VMEM((2, ROW, 128), BF16), pltpu.VMEM((2, ROW, 128), BF16), pltpu.VMEM((2, ROW, 128), BF16),
            pltpu.VMEM((128, ROW), BF16),
            pltpu.VMEM((128, ROW), F32), pltpu.VMEM((128, ROW), F32),
        ],
        compiler_params=pltpu.CompilerParams(vmem_limit_bytes=LIMIT),
        name="attention",
    )(qh, kh, vh, dh, ser, var, variate_bias)
    tokens = sds((TOK, D), BF16)
    mixed, dq, dk, dv, wg, bg = pl.pallas_call(
        return_kernel,
        out_shape=[tokens] * 4 + [sds((16, D), F32), sds((8, 128), F32)],
        in_specs=[VM] * 7,
        out_specs=[VM] * 6,
        scratch_shapes=[
            pltpu.VMEM((TOK, D), BF16),
            pltpu.VMEM((NX, NZ, NC, 16, D), BF16), pltpu.VMEM((NX, NZ, 16, D), BF16),
            pltpu.VMEM((4, NX, 16, D), BF16), pltpu.VMEM((3, NX, 16, D), BF16),
            pltpu.VMEM((4, NX, 16, D), BF16), pltpu.VMEM((3, NX, 16, D), BF16),
            pltpu.VMEM((NX, 16, D), F32), pltpu.VMEM((NX, 16, D), BF16), pltpu.VMEM((NX, 16, D), BF16),
            pltpu.VMEM((16, D), F32), pltpu.VMEM((8, 16, 128), F32),
            pltpu.VMEM((3, 8, 128), F32), pltpu.VMEM((18, 8, 128), F32),
            DMA((4, 8)), DMA((4, 8)), DMA((4,)),
            DMA((8,)), DMA((8,)),
            DMA((2, 4)), DMA((2, 4)),
            DMA((4,)), DMA((4,)),
            DMA((2, 8)), DMA((2, 8)),
            DMA((18,)), DMA((18,)),
        ],
        compiler_params=pltpu.CompilerParams(collective_id=1, has_side_effects=True, vmem_limit_bytes=LIMIT),
        name="giveback",
    )(ctxh, dqh, dkh, dvh, bt, d_mixed[0], wf)
    return mixed[None], dq[None], dk[None], dv[None], wg, bg[:2, :HEADS]


def solution(mesh):
    finer = Mesh(mesh.devices.reshape(NY, NX, NZ, NC), ("ctx", "x", "z", "core"))
    tokens = P(DP, "ctx", None)
    ids = P(DP, "ctx")
    return jax.shard_map(
        on_device,
        mesh=finer,
        in_specs=(tokens, tokens, tokens, tokens, ids, ids, P(), P(DP, None)),
        out_specs=(tokens, tokens, tokens, tokens, P(DP, None), P()),
        check_vma=False,
    )
```

```python
import functools

import jax
import jax.numpy as jnp
from jax import lax
from jax.experimental import pallas as pl
from jax.experimental.pallas import tpu as pltpu
from jax.sharding import Mesh
from jax.sharding import PartitionSpec as P

HEADS = 16
HEAD_DIM = 64
NY, NX, NZ, NC = 8, 4, 8, 2
TOK = 128
ROW = 1024
D = 1024
DP = ("x", "z", "core")
MESH = pl.DeviceIdType.MESH
F32 = jnp.float32
BF16 = jnp.bfloat16
ORDER = (1, 7, 2, 6, 3, 5, 4)
MASK = 2048.0
BQ = 256


def remote(src, dst, ssem, rsem, **where):
    return pltpu.make_async_remote_copy(
        src_ref=src, dst_ref=dst, send_sem=ssem, recv_sem=rsem,
        device_id=where, device_id_type=MESH,
    )


def meet(peers):
    sem = pltpu.get_barrier_semaphore()
    for peer in peers:
        pl.semaphore_signal(sem, inc=1, device_id=peer, device_id_type=MESH)
    pl.semaphore_wait(sem, len(peers))


def others(axis, n):
    me = lax.axis_index(axis)
    return [{axis: lax.rem(me + d, n)} for d in range(1, n)]


def span(i, n=128):
    return pl.ds(pl.multiple_of(i * n, n), n)


def spread(src, dst, ssem, rsem, lsem):
    me = lax.axis_index("ctx")
    copies = []
    for d in ORDER:
        to = lax.rem(me + d, NY)
        c = remote(src.at[:, span(to)], dst.at[span(me), :], ssem.at[d], rsem.at[d], ctx=to)
        c.start()
        copies.append(c)
    c = pltpu.make_async_copy(src.at[:, span(me)], dst.at[span(me), :], lsem)
    c.start()
    copies.append(c)
    return copies


def unspread(src, dst, ssem, rsem, lsem):
    me = lax.axis_index("ctx")
    copies = []
    for d in ORDER:
        to = lax.rem(me + d, NY)
        c = remote(src.at[span(to), :], dst.at[:, span(me)], ssem.at[d], rsem.at[d], ctx=to)
        c.start()
        copies.append(c)
    c = pltpu.make_async_copy(src.at[span(me), :], dst.at[:, span(me)], lsem)
    c.start()
    copies.append(c)
    return copies


def fused_kernel(q, k, v, dm, ser, var, w, bias,
                 mixed, dq, dk, dv, wg, bg,
                 qh, kh, vh, dh, ser_o, var_o, wf, dctx,
                 base_s, qa_s, ka_s, va_s, qt_s, eb_s, ds_s, c_s32, inv_s, dn_s, dnt_s, dkt, dvt,
                 ctxh, dqh, dkh, dvh,
                 ctx, g, sa, sb_r, sb_l, rr, rl, acc, xs, xr, ys, yr, bs, br,
                 a_s, a_r, a_l, i_s, i_r, i_l, wx_s, wx_r, wz_s, wz_r, wc_s, wc_r, w_l,
                 c_s, c_r, z_s, z_r, x_s, x_r, y_s, y_r, b_s, b_r):
    y, x, z, c = (lax.axis_index(a) for a in ("ctx", "x", "z", "core"))
    sib = 1 - c
    up, down = lax.rem(z + 1, NZ), lax.rem(z + NZ - 1, NZ)
    meet(others("ctx", NY) + others("x", NX) + others("z", NZ) + [{"core": sib}])

    own = pltpu.make_async_copy(w, wf.at[x, z, c], w_l)
    own.start()
    x_copies = []
    for d in range(1, NX):
        cp = remote(w, wf.at[x, z, c], wx_s.at[d], wx_r.at[d], x=lax.rem(x + d, NX))
        cp.start()
        x_copies.append(cp)
    ids = []
    for n, (src, dst) in enumerate(((ser, ser_o), (var, var_o))):
        for d in ORDER:
            cp = remote(src, dst.at[:, span(y)], i_s.at[n, d], i_r.at[n, d], ctx=lax.rem(y + d, NY))
            cp.start()
            ids.append(cp)
        cp = pltpu.make_async_copy(src, dst.at[:, span(y)], i_l.at[n])
        cp.start()
        ids.append(cp)
    ins = []
    for n, (src, dst) in enumerate(((q, qh), (k, kh), (v, vh))):
        ins.append(spread(src, dst, a_s.at[n], a_r.at[n], a_l.at[n]))

    own.wait()
    arrived = {}
    siblings = []
    sub = [lax.rem(x + NX - j, NX) for j in range(NX)]

    def block(zz, j):
        return wf.at[sub[j], zz, c]

    def to_sibling(zz, j, n):
        cp = remote(block(zz, j), block(zz, j), wc_s.at[n, j], wc_r.at[n, j], core=sib)
        cp.start()
        siblings.append(cp)

    for s in range(4):
        zr, zl = lax.rem(z + NZ - s, NZ), lax.rem(z + s, NZ)
        for j in range(NX):
            if s == 0:
                if j > 0:
                    x_copies[j - 1].wait()
            else:
                arrived[(0, s - 1, j)].wait()
            cp = remote(block(zr, j), block(zr, j), wz_s.at[0, s, j], wz_r.at[0, s, j], z=up)
            cp.start()
            arrived[(0, s, j)] = cp
            if s < 3:
                if s > 0:
                    arrived[(1, s - 1, j)].wait()
                cp = remote(block(zl, j), block(zl, j), wz_s.at[1, s, j], wz_r.at[1, s, j], z=down)
                cp.start()
                arrived[(1, s, j)] = cp
            to_sibling(zr, j, s)
            if 0 < s < 3:
                to_sibling(zl, j, 4 + s)
    zr, zl = lax.rem(z + NZ - 4, NZ), lax.rem(z + 3, NZ)
    for j in range(NX):
        arrived[(1, 2, j)].wait()
        to_sibling(zl, j, 7)
        arrived[(0, 3, j)].wait()
        to_sibling(zr, j, 4)
    for cp in siblings:
        cp.wait()
    for xi in range(NX):
        rows = wf[xi].reshape(256, D)
        got = lax.dot_general(dm[...], rows, (((1,), (1,)), ((), ())), preferred_element_type=F32)
        dctx[:, 256 * xi:256 * (xi + 1)] = got.astype(BF16)
    ins.append(spread(dctx, dh, a_s.at[3], a_r.at[3], a_l.at[3]))

    for cp in ids + ins[0] + ins[1]:
        cp.wait()
    feat = lax.broadcasted_iota(jnp.int32, (128, ROW), 0) % 64
    held = jnp.where(feat < 16, ser_o[...], var_o[...])
    want = jnp.where(feat < 16, feat, jnp.where(feat < 28, feat % 4, -1))
    base = jnp.where(held == want, 1.0, 0.0).T
    base_s[...] = base
    lane = lax.broadcasted_iota(jnp.int32, (1, 128), 1)
    within = lane % 64
    half = [slice(0, 64), slice(64, 128)]
    mine = [lane < 64, lane >= 64]
    qt_s[...] = (qh[...].astype(F32) * 0.125).T.astype(BF16)
    for h in range(2):
        gap = jnp.full((1, 128), bias[0, 2 * y + h] - bias[1, 2 * y + h], F32)
        hi = gap.astype(BF16).astype(F32)
        mid = (gap - hi).astype(BF16).astype(F32)
        low = gap - hi - mid
        coef = jnp.where(within < 16, MASK, jnp.where(within < 20, hi, jnp.where(within < 24, mid, low)))
        qa_s[h] = jnp.where(mine[h], qh[...].astype(F32) * 0.125, base * coef).astype(BF16)
        ka_s[h] = jnp.where(mine[h], kh[...].astype(F32), base).astype(BF16)
    for cp in ins[2]:
        cp.wait()
    for h in range(2):
        va_s[h] = jnp.where(mine[h], vh[...].astype(F32), 1.0).astype(BF16)

    def forward(i, carry):
        rows = span(i, BQ)
        un = []
        for h in range(2):
            s = lax.dot_general(qa_s[h, rows, :], ka_s[h], (((1,), (1,)), ((), ())),
                                preferred_element_type=F32)
            top = jnp.max(s, axis=1, keepdims=True)
            e = jnp.exp(s - top).astype(BF16)
            eb_s[h, rows, :] = e
            un.append(jnp.dot(e, va_s[h], preferred_element_type=F32))
        inv = 1.0 / pltpu.roll(jnp.where(mine[0], un[1], un[0]), 64, 1)
        mix = jnp.where(mine[0], un[0], un[1]) * inv
        inv_s[rows, :] = inv
        c_s32[rows, :] = mix
        ctxh[rows, :] = mix.astype(BF16)
        return carry

    lax.fori_loop(0, ROW // BQ, forward, 0)
    back = [unspread(ctxh, ctx, a_s.at[4], a_r.at[4], a_l.at[4])]

    for cp in ins[3]:
        cp.wait()
    dn_s[...] = (dh[...].astype(F32) * inv_s[...]).astype(BF16)
    dnt_s[...] = dn_s[...].astype(F32).T.astype(BF16)

    def values_grad(j, carry):
        cols = span(j, 256)
        for h in range(2):
            dvt[half[h], :] = jnp.dot(dnt_s[half[h], :], eb_s[h, :, cols], preferred_element_type=F32)
        dvh[cols, :] = dvt[...].T.astype(BF16)
        return carry

    lax.fori_loop(0, ROW // 256, values_grad, 0)
    back.append(unspread(dvh, dv, a_s.at[5], a_r.at[5], a_l.at[5]))

    def queries_grad(i, carry):
        rows = span(i, BQ)
        dnf = dn_s[rows, :].astype(F32)
        prod = dnf * c_s32[rows, :]
        o_blk = base_s[rows, :]
        outs, sums = [], []
        for h in range(2):
            delta = jnp.sum(jnp.where(mine[h], prod, 0.0), axis=1, keepdims=True)
            hi = delta.astype(BF16).astype(F32)
            mid = (delta - hi).astype(BF16).astype(F32)
            low = delta - hi - mid
            da = jnp.where(within == 0, -hi, jnp.where(within == 1, -mid, jnp.where(within == 2, -low, 0.0)))
            da = jnp.where(mine[h], dnf, da).astype(BF16)
            t = lax.dot_general(da, va_s[h], (((1,), (1,)), ((), ())), preferred_element_type=F32)
            ds = (eb_s[h, rows, :].astype(F32) * t).astype(BF16)
            ds_s[h, rows, :] = ds
            got = jnp.dot(ds, ka_s[h], preferred_element_type=F32)
            u = jnp.where(mine[1 - h] & (within >= 16) & (within < 20), got, 0.0)
            sums.append(jnp.sum(u * o_blk, axis=0, keepdims=True))
            sums.append(jnp.sum(u * (1.0 - o_blk), axis=0, keepdims=True))
            outs.append(got)
        dqh[rows, :] = (jnp.where(mine[0], outs[0], outs[1]) * 0.125).astype(BF16)
        return tuple(a + b for a, b in zip(carry, sums))

    zero = jnp.zeros((1, 128), F32)
    sums = lax.fori_loop(0, ROW // BQ, queries_grad, (zero,) * 4)
    back.append(unspread(dqh, dq, a_s.at[6], a_r.at[6], a_l.at[6]))
    total = [jnp.sum(a, axis=1, keepdims=True) for a in sums]
    row = lax.broadcasted_iota(jnp.int32, (8, 128), 0)
    col = lax.broadcasted_iota(jnp.int32, (8, 128), 1) - 2 * y
    tile = jnp.zeros((8, 128), F32)
    for h in range(2):
        for r in range(2):
            tile = jnp.where((row == r) & (col == h), total[2 * h + r], tile)
    bs[3] = tile
    bsib = remote(bs.at[3], br.at[0], b_s.at[0], b_r.at[0], core=sib)
    bsib.start()

    for cp in back[0]:
        cp.wait()
    for xi in range(NX):
        part = ctx[:, 256 * xi:256 * (xi + 1)].astype(F32).T.astype(BF16)
        got = jnp.dot(part, dm[...], preferred_element_type=F32)
        g[xi] = got.astype(BF16).reshape(8, 2, 16, D)
    sibs = {}
    for off in (4, 5, 3, 6, 2, 7, 1, 0):
        zt = lax.rem(z + off, NZ)
        cp = remote(g.at[:, zt, sib], sa.at[:, zt], c_s.at[off], c_r.at[off], core=sib)
        cp.start()
        sibs[off] = cp

    def keys_grad(j, carry):
        cols = span(j, 256)
        for h in range(2):
            dkt[half[h], :] = jnp.dot(qt_s[half[h], :], ds_s[h, :, cols], preferred_element_type=F32)
        dkh[cols, :] = dkt[...].T.astype(BF16)
        return carry

    lax.fori_loop(0, ROW // 256, keys_grad, 0)
    back.append(unspread(dkh, dk, a_s.at[7], a_r.at[7], a_l.at[7]))

    bsib.wait()
    bs[0] = bs[3] + br[0]
    bz = []
    for d in range(1, NZ):
        cp = remote(bs.at[0], br.at[d], b_s.at[d], b_r.at[d], z=lax.rem(z + d, NZ))
        cp.start()
        bz.append(cp)

    def part_sum(off):
        zt = lax.rem(z + off, NZ)
        sibs[off].wait()
        return g[:, zt, c].astype(F32) + sa[:, zt].astype(F32)

    r_cp, l_cp = [], []
    for s in range(4):
        val = part_sum(4 - s)
        if s > 0:
            r_cp[s - 1].wait()
            val = val + rr[s - 1].astype(F32)
        sb_r[s] = val.astype(BF16)
        cp = remote(sb_r.at[s], rr.at[s], z_s.at[0, s], z_r.at[0, s], z=up)
        cp.start()
        r_cp.append(cp)
        if s < 3:
            val = part_sum(5 + s)
            if s > 0:
                l_cp[s - 1].wait()
                val = val + rl[s - 1].astype(F32)
            sb_l[s] = val.astype(BF16)
            cp = remote(sb_l.at[s], rl.at[s], z_s.at[1, s], z_r.at[1, s], z=down)
            cp.start()
            l_cp.append(cp)
        got = jnp.dot(ctx[...], wf[...].reshape(D, D)[:, 256 * s:256 * (s + 1)], preferred_element_type=F32)
        mixed[:, 256 * s:256 * (s + 1)] = got.astype(BF16)
    own = part_sum(0)
    for cp in bz:
        cp.wait()
    tile = bs[0]
    for d in range(1, NZ):
        tile = tile + br[d]
    bs[1] = tile
    bx = []
    for d in range(1, NX):
        cp = remote(bs.at[1], br.at[7 + d], b_s.at[7 + d], b_r.at[7 + d], x=lax.rem(x + d, NX))
        cp.start()
        bx.append(cp)
    l_cp[2].wait()
    r_cp[3].wait()
    own = own + rl[2].astype(F32) + rr[3].astype(F32)
    acc[...] = own
    xs[...] = own.astype(BF16)
    xcp = []
    for d in range(1, NX):
        to = lax.rem(x + d, NX)
        cp = remote(xs.at[to], xr.at[d], x_s.at[d], x_r.at[d], x=to)
        cp.start()
        xcp.append(cp)
    for cp in bx:
        cp.wait()
    bs[2] = bs[1] + br[8] + br[9] + br[10]
    by = []
    for d in range(1, NY):
        cp = remote(bs.at[2], br.at[10 + d], b_s.at[10 + d], b_r.at[10 + d], ctx=lax.rem(y + d, NY))
        cp.start()
        by.append(cp)
    for cp in xcp:
        cp.wait()
    ys[...] = acc[x] + xr[1].astype(F32) + xr[2].astype(F32) + xr[3].astype(F32)
    ycp = []
    for d in ORDER:
        to = lax.rem(y + d, NY)
        cp = remote(ys.at[:, span(to)], yr.at[d], y_s.at[0, d], y_r.at[0, d], ctx=to)
        cp.start()
        ycp.append(cp)
    for cp in by:
        cp.wait()
    tile = bs[2]
    for d in range(1, NY):
        tile = tile + br[10 + d]
    bg[...] = tile
    for cp in ycp:
        cp.wait()
    piece = ys[:, span(y)]
    for d in range(1, NY):
        piece = piece + yr[d]
    yr[0] = piece
    wg[:, span(y)] = piece
    last = []
    for d in ORDER:
        to = lax.rem(y + d, NY)
        cp = remote(yr.at[0], wg.at[:, span(y)], y_s.at[1, d], y_r.at[1, d], ctx=to)
        cp.start()
        last.append(cp)
    for cp in last + back[1] + back[2] + back[3]:
        cp.wait()


def finish_kernel(*refs):
    for src, dst in zip(refs[:6], refs[6:]):
        dst[...] = src[:dst.shape[0], :dst.shape[1]]


VM = pl.BlockSpec(memory_space=pltpu.VMEM)
SM = pl.BlockSpec(memory_space=pltpu.SMEM)
ANY = pl.BlockSpec(memory_space=pl.ANY)
DMA = pltpu.SemaphoreType.DMA
LIMIT = 62 * 1024 * 1024


def sds(shape, dtype):
    return jax.ShapeDtypeStruct(shape, dtype)


def on_device(queries, keys, values, d_mixed, series_ids, variate_ids, variate_bias, w_out):
    tokens = sds((TOK, D), BF16)
    wide = pltpu.VMEM((ROW, 128), BF16)
    wide32 = pltpu.VMEM((ROW, 128), F32)
    pair = pltpu.VMEM((2, ROW, 128), BF16)
    square = pltpu.VMEM((2, ROW, ROW), BF16)
    results = pl.pallas_call(
        fused_kernel,
        out_shape=[tokens] * 4 + [sds((16, D), F32), sds((8, 128), F32)],
        in_specs=[ANY] * 3 + [VM] * 4 + [SM],
        out_specs=[VM] * 6,
        scratch_shapes=[
            wide, wide, wide, wide,
            pltpu.VMEM((1, ROW), jnp.int32), pltpu.VMEM((1, ROW), jnp.int32),
            pltpu.VMEM((NX, NZ, NC, 16, D), BF16), pltpu.VMEM((TOK, D), BF16),
            wide32, pair, pair, pair, pltpu.VMEM((128, ROW), BF16),
            square, square, wide32, wide32, wide, pltpu.VMEM((128, ROW), BF16),
            pltpu.VMEM((128, 256), F32), pltpu.VMEM((128, 256), F32),
            wide, wide, wide, wide,
            pltpu.VMEM((TOK, D), BF16),
            pltpu.VMEM((NX, NZ, NC, 16, D), BF16), pltpu.VMEM((NX, NZ, 16, D), BF16),
            pltpu.VMEM((4, NX, 16, D), BF16), pltpu.VMEM((3, NX, 16, D), BF16),
            pltpu.VMEM((4, NX, 16, D), BF16), pltpu.VMEM((3, NX, 16, D), BF16),
            pltpu.VMEM((NX, 16, D), F32), pltpu.VMEM((NX, 16, D), BF16), pltpu.VMEM((NX, 16, D), BF16),
            pltpu.VMEM((16, D), F32), pltpu.VMEM((8, 16, 128), F32),
            pltpu.VMEM((4, 8, 128), F32), pltpu.VMEM((18, 8, 128), F32),
            DMA((8, 8)), DMA((8, 8)), DMA((8,)),
            DMA((2, 8)), DMA((2, 8)), DMA((2,)),
            DMA((4,)), DMA((4,)),
            DMA((2, 4, 4)), DMA((2, 4, 4)),
            DMA((8, 4)), DMA((8, 4)), DMA,
            DMA((8,)), DMA((8,)),
            DMA((2, 4)), DMA((2, 4)),
            DMA((4,)), DMA((4,)),
            DMA((2, 8)), DMA((2, 8)),
            DMA((18,)), DMA((18,)),
        ],
        compiler_params=pltpu.CompilerParams(collective_id=0, has_side_effects=True, vmem_limit_bytes=LIMIT),
        name="fused",
    )(queries[0], keys[0], values[0], d_mixed[0], series_ids, variate_ids, w_out, variate_bias)
    mixed, dq, dk, dv, wg, bg = pl.pallas_call(
        finish_kernel,
        out_shape=[tokens] * 4 + [sds((16, D), F32), sds((2, HEADS), F32)],
        in_specs=[VM] * 6,
        out_specs=[VM] * 6,
        compiler_params=pltpu.CompilerParams(vmem_limit_bytes=LIMIT),
        name="finish",
    )(*results)
    return mixed[None], dq[None], dk[None], dv[None], wg, bg


def solution(mesh):
    finer = Mesh(mesh.devices.reshape(NY, NX, NZ, NC), ("ctx", "x", "z", "core"))
    tokens = P(DP, "ctx", None)
    ids = P(DP, "ctx")
    return jax.shard_map(
        on_device,
        mesh=finer,
        in_specs=(tokens, tokens, tokens, tokens, ids, ids, P(), P(DP, None)),
        out_specs=(tokens, tokens, tokens, tokens, P(DP, None), P()),
        check_vma=False,
    )
```

```python
import functools

import jax
import jax.numpy as jnp
from jax import lax
from jax.experimental import pallas as pl
from jax.experimental.pallas import tpu as pltpu
from jax.sharding import Mesh
from jax.sharding import PartitionSpec as P

HEADS = 16
HEAD_DIM = 64
NY, NX, NZ, NC = 8, 4, 8, 2
TOK = 128
ROW = 1024
D = 1024
DP = ("x", "z", "core")
MESH = pl.DeviceIdType.MESH
F32 = jnp.float32
BF16 = jnp.bfloat16
ORDER = (1, 7, 2, 6, 3, 5, 4)
LATE = (4, 5, 3, 6, 2, 7, 1, 0)
MASK = 2048.0
BQ = 256


def remote(src, dst, ssem, rsem, **where):
    return pltpu.make_async_remote_copy(
        src_ref=src, dst_ref=dst, send_sem=ssem, recv_sem=rsem,
        device_id=where, device_id_type=MESH,
    )


def meet(peers):
    sem = pltpu.get_barrier_semaphore()
    for peer in peers:
        pl.semaphore_signal(sem, inc=1, device_id=peer, device_id_type=MESH)
    pl.semaphore_wait(sem, len(peers))


def others(axis, n):
    me = lax.axis_index(axis)
    return [{axis: lax.rem(me + d, n)} for d in range(1, n)]


def span(i, n=128):
    return pl.ds(pl.multiple_of(i * n, n), n)


def spread(src, dst, ssem, rsem, lsem):
    me = lax.axis_index("ctx")
    copies = []
    for d in ORDER:
        to = lax.rem(me + d, NY)
        c = remote(src.at[:, span(to)], dst.at[span(me), :], ssem.at[d], rsem.at[d], ctx=to)
        c.start()
        copies.append(c)
    c = pltpu.make_async_copy(src.at[:, span(me)], dst.at[span(me), :], lsem)
    c.start()
    copies.append(c)
    return copies


def unspread(src, dst, ssem, rsem, lsem):
    me = lax.axis_index("ctx")
    copies = []
    for d in ORDER:
        to = lax.rem(me + d, NY)
        c = remote(src.at[span(to), :], dst.at[:, span(me)], ssem.at[d], rsem.at[d], ctx=to)
        c.start()
        copies.append(c)
    c = pltpu.make_async_copy(src.at[span(me), :], dst.at[:, span(me)], lsem)
    c.start()
    copies.append(c)
    return copies


def fused_kernel(q, k, v, dm_in, ser, var, w, bias,
                 mixed_o, dq, dk, dv, wg, bg,
                 dm, mixed, qh, kh, vh, dh, ser_o, var_o, wf, dctx,
                 base_s, qa_s, ka_s, va_s, qt_s, eb_s, ds_s, c_s32, inv_s, dn_s, dnt_s, dkt, dvt,
                 ctxh, dqh, dkh, dvh,
                 ctx, g, sa, hs, hf, hr, zs, zr, ys, yr, bs, br,
                 a_s, a_r, a_l, i_s, i_r, i_l, wz_s, wz_r, wx_s, wx_r, wc_s, wc_r, w_l,
                 c_s, c_r, x_s, x_r, z_s, z_r, y_s, y_r, b_s, b_r):
    y, x, z, c = (lax.axis_index(a) for a in ("ctx", "x", "z", "core"))
    sib = 1 - c
    dm_copy = pltpu.make_async_copy(dm_in, dm, w_l.at[1])
    dm_copy.start()
    own = pltpu.make_async_copy(w, wf.at[x, z, c], w_l.at[0])
    own.start()
    meet(others("ctx", NY) + others("x", NX) + others("z", NZ) + [{"core": sib}])

    from_z, from_x = {}, {}
    for d in ORDER:
        cp = remote(w, wf.at[x, z, c], wz_s.at[d], wz_r.at[d], z=lax.rem(z + d, NZ))
        cp.start()
        from_z[d] = cp

    def to_x(e):
        src = wf.at[x, lax.rem(z + NZ - e, NZ), c]
        for d in range(1, NX):
            cp = remote(w if e == 0 else src, src, wx_s.at[e, d], wx_r.at[e, d], x=lax.rem(x + d, NX))
            cp.start()
            from_x[e, d] = cp

    to_x(0)
    ids = []
    for n, (src, dst) in enumerate(((ser, ser_o), (var, var_o))):
        for d in ORDER:
            cp = remote(src, dst.at[:, span(y)], i_s.at[n, d], i_r.at[n, d], ctx=lax.rem(y + d, NY))
            cp.start()
            ids.append(cp)
        cp = pltpu.make_async_copy(src, dst.at[:, span(y)], i_l.at[n])
        cp.start()
        ids.append(cp)
    ins = []
    for n, (src, dst) in enumerate(((q, qh), (k, kh), (v, vh))):
        ins.append(spread(src, dst, a_s.at[n], a_r.at[n], a_l.at[n]))

    own.wait()
    siblings = []

    def to_sibling(e):
        for d in range(1, NX):
            from_x[e, d].wait()
        part = wf.at[:, lax.rem(z + NZ - e, NZ), c]
        cp = remote(part, part, wc_s.at[e], wc_r.at[e], core=sib)
        cp.start()
        siblings.append(cp)

    for e in ORDER:
        from_z[e].wait()
        to_x(e)

    for cp in ids + ins[0] + ins[1]:
        cp.wait()
    feat = lax.broadcasted_iota(jnp.int32, (128, ROW), 0) % 64
    held = jnp.where(feat < 16, ser_o[...], var_o[...])
    want = jnp.where(feat < 16, feat, jnp.where(feat < 28, feat % 4, -1))
    base = jnp.where(held == want, 1.0, 0.0).T
    base_s[...] = base
    lane = lax.broadcasted_iota(jnp.int32, (1, 128), 1)
    within = lane % 64
    half = [slice(0, 64), slice(64, 128)]
    mine = [lane < 64, lane >= 64]
    qt_s[...] = (qh[...].astype(F32) * 0.125).T.astype(BF16)
    for h in range(2):
        gap = jnp.full((1, 128), bias[0, 2 * y + h] - bias[1, 2 * y + h], F32)
        hi = gap.astype(BF16).astype(F32)
        mid = (gap - hi).astype(BF16).astype(F32)
        low = gap - hi - mid
        coef = jnp.where(within < 16, MASK, jnp.where(within < 20, hi, jnp.where(within < 24, mid, low)))
        qa_s[h] = jnp.where(mine[h], qh[...].astype(F32) * 0.125, base * coef).astype(BF16)
        ka_s[h] = jnp.where(mine[h], kh[...].astype(F32), base).astype(BF16)
    def scores(i, carry):
        rows = span(i, BQ)
        for h in range(2):
            s = lax.dot_general(qa_s[h, rows, :], ka_s[h], (((1,), (1,)), ((), ())),
                                preferred_element_type=F32)
            top = jnp.max(s, axis=1, keepdims=True)
            eb_s[h, rows, :] = jnp.exp(s - top).astype(BF16)
        return carry

    lax.fori_loop(0, ROW // BQ, scores, 0)
    for e in (0,) + ORDER:
        to_sibling(e)
    for cp in ins[2]:
        cp.wait()
    for h in range(2):
        va_s[h] = jnp.where(mine[h], vh[...].astype(F32), 1.0).astype(BF16)

    def forward(i, carry):
        rows = span(i, BQ)
        un = [jnp.dot(eb_s[h, rows, :], va_s[h], preferred_element_type=F32) for h in range(2)]
        inv = 1.0 / pltpu.roll(jnp.where(mine[0], un[1], un[0]), 64, 1)
        mix = jnp.where(mine[0], un[0], un[1]) * inv
        inv_s[rows, :] = inv
        c_s32[rows, :] = mix
        ctxh[rows, :] = mix.astype(BF16)
        return carry

    lax.fori_loop(0, ROW // BQ, forward, 0)
    back = [unspread(ctxh, ctx, a_s.at[4], a_r.at[4], a_l.at[4])]

    for cp in siblings:
        cp.wait()
    dm_copy.wait()
    for xi in range(NX):
        rows = wf[xi].reshape(256, D)
        got = lax.dot_general(dm[...], rows, (((1,), (1,)), ((), ())), preferred_element_type=F32)
        dctx[:, 256 * xi:256 * (xi + 1)] = got.astype(BF16)
    ins.append(spread(dctx, dh, a_s.at[3], a_r.at[3], a_l.at[3]))

    for cp in back[0]:
        cp.wait()
    for xi in range(NX):
        part = ctx[:, 256 * xi:256 * (xi + 1)].astype(F32).T.astype(BF16)
        got = jnp.dot(part, dm[...], preferred_element_type=F32)
        g[xi] = got.astype(BF16).reshape(8, 2, 16, D)
    sibs = {}
    for off in LATE:
        zt = lax.rem(z + off, NZ)
        cp = remote(g.at[:, zt, sib], sa.at[:, zt], c_s.at[off], c_r.at[off], core=sib)
        cp.start()
        sibs[off] = cp

    xcp, zcp = {}, []

    def sum_cores(off):
        zt = lax.rem(z + off, NZ)
        sibs[off].wait()
        val = g[:, zt, c].astype(F32) + sa[:, zt].astype(F32)
        hf[off] = val
        hs[off] = val.astype(BF16)
        for d in range(1, NX):
            to = lax.rem(x + d, NX)
            cp = remote(hs.at[off, to], hr.at[off, d], x_s.at[off, d], x_r.at[off, d], x=to)
            cp.start()
            xcp[off, d] = cp

    ins[3][-1].wait()

    def queries_grad(n, carry):
        pair = []
        for m in range(2):
            at = 2 * n + m
            odd = at % 2
            d = odd * ((at + 1) // 2) + (1 - odd) * ((NY - at // 2) % NY)
            to = lax.rem(y + d, NY)
            cp = remote(dctx.at[:, span(to)], dh.at[span(y), :], a_s.at[3, d], a_r.at[3, d], ctx=to)
            if m:
                cp.wait()
            else:
                pl.when(n > 0)(cp.wait)
            pair.append(span(lax.rem(y + NY - d, NY)))

        def both(ref, *lead):
            return jnp.concatenate([ref[(*lead, r, slice(None))] for r in pair], axis=0)

        def keep(ref, val, *lead):
            for m in range(2):
                ref[(*lead, pair[m], slice(None))] = val[128 * m:128 * (m + 1)]

        dn = (both(dh).astype(F32) * both(inv_s)).astype(BF16)
        keep(dn_s, dn)
        dnf = dn.astype(F32)
        prod = dnf * both(c_s32)
        o_blk = both(base_s)
        outs, sums = [], []
        for h in range(2):
            delta = jnp.sum(jnp.where(mine[h], prod, 0.0), axis=1, keepdims=True)
            hi = delta.astype(BF16).astype(F32)
            mid = (delta - hi).astype(BF16).astype(F32)
            low = delta - hi - mid
            da = jnp.where(within == 0, -hi, jnp.where(within == 1, -mid, jnp.where(within == 2, -low, 0.0)))
            da = jnp.where(mine[h], dnf, da).astype(BF16)
            t = lax.dot_general(da, va_s[h], (((1,), (1,)), ((), ())), preferred_element_type=F32)
            ds = (both(eb_s, h).astype(F32) * t).astype(BF16)
            keep(ds_s, ds, h)
            got = jnp.dot(ds, ka_s[h], preferred_element_type=F32)
            u = jnp.where(mine[1 - h] & (within >= 16) & (within < 20), got, 0.0)
            sums.append(jnp.sum(u * o_blk, axis=0, keepdims=True))
            sums.append(jnp.sum(u * (1.0 - o_blk), axis=0, keepdims=True))
            outs.append(got)
        keep(dqh, (jnp.where(mine[0], outs[0], outs[1]) * 0.125).astype(BF16))
        return tuple(a + b for a, b in zip(carry, sums))

    zero = jnp.zeros((1, 128), F32)
    sums = lax.fori_loop(0, 2, queries_grad, (zero,) * 4)
    for off in LATE[:4]:
        sum_cores(off)
    sums = lax.fori_loop(2, 4, queries_grad, sums)
    back.append(unspread(dqh, dq, a_s.at[6], a_r.at[6], a_l.at[6]))
    for off in LATE[4:]:
        sum_cores(off)
    dnt_s[...] = dn_s[...].astype(F32).T.astype(BF16)

    def values_grad(j, carry):
        cols = span(j, 256)
        for h in range(2):
            dvt[half[h], :] = jnp.dot(dnt_s[half[h], :], eb_s[h, :, cols], preferred_element_type=F32)
        dvh[cols, :] = dvt[...].T.astype(BF16)
        return carry

    lax.fori_loop(0, ROW // 256, values_grad, 0)
    back.append(unspread(dvh, dv, a_s.at[5], a_r.at[5], a_l.at[5]))
    total = [jnp.sum(a, axis=1, keepdims=True) for a in sums]
    row = lax.broadcasted_iota(jnp.int32, (8, 128), 0)
    col = lax.broadcasted_iota(jnp.int32, (8, 128), 1) - 2 * y
    tile = jnp.zeros((8, 128), F32)
    for h in range(2):
        for r in range(2):
            tile = jnp.where((row == r) & (col == h), total[2 * h + r], tile)
    bs[3] = tile
    bsib = remote(bs.at[3], br.at[0], b_s.at[0], b_r.at[0], core=sib)
    bsib.start()

    def keys_grad(j, carry):
        cols = span(j, 256)
        for h in range(2):
            dkt[half[h], :] = jnp.dot(qt_s[half[h], :], ds_s[h, :, cols], preferred_element_type=F32)
        dkh[cols, :] = dkt[...].T.astype(BF16)
        return carry

    lax.fori_loop(0, ROW // 256, keys_grad, 0)
    back.append(unspread(dkh, dk, a_s.at[7], a_r.at[7], a_l.at[7]))

    for n in range(4):
        cols = slice(256 * n, 256 * (n + 1))
        got = jnp.dot(ctx[...], wf[...].reshape(D, D)[:, cols], preferred_element_type=F32)
        mixed[:, cols] = got.astype(BF16)
    mixed_copy = pltpu.make_async_copy(mixed, mixed_o, w_l.at[0])
    mixed_copy.start()
    bsib.wait()
    bs[0] = bs[3] + br[0]
    bz = []
    for d in range(1, NZ):
        cp = remote(bs.at[0], br.at[d], b_s.at[d], b_r.at[d], z=lax.rem(z + d, NZ))
        cp.start()
        bz.append(cp)

    for off in LATE:
        for d in range(1, NX):
            xcp[off, d].wait()
        val = hf[off, x] + hr[off, 1].astype(F32) + hr[off, 2].astype(F32) + hr[off, 3].astype(F32)
        if off:
            zs[off] = val.astype(BF16)
            cp = remote(zs.at[off], zr.at[off], z_s.at[off], z_r.at[off], z=lax.rem(z + off, NZ))
            cp.start()
            zcp.append(cp)
        if off == 4:
            for cp in bz:
                cp.wait()
            tile = bs[0]
            for d in range(1, NZ):
                tile = tile + br[d]
            bs[1] = tile
            bx = []
            for d in range(1, NX):
                cp = remote(bs.at[1], br.at[7 + d], b_s.at[7 + d], b_r.at[7 + d], x=lax.rem(x + d, NX))
                cp.start()
                bx.append(cp)
    for cp in bx:
        cp.wait()
    bs[2] = bs[1] + br[8] + br[9] + br[10]
    by = []
    for d in range(1, NY):
        cp = remote(bs.at[2], br.at[10 + d], b_s.at[10 + d], b_r.at[10 + d], ctx=lax.rem(y + d, NY))
        cp.start()
        by.append(cp)
    for cp in zcp:
        cp.wait()
    for d in range(1, NZ):
        val = val + zr[d].astype(F32)
    ys[...] = val.astype(BF16)
    ycp = []
    for d in ORDER:
        cp = remote(ys, yr.at[d], y_s.at[d], y_r.at[d], ctx=lax.rem(y + d, NY))
        cp.start()
        ycp.append(cp)
    for cp in by:
        cp.wait()
    tile = bs[2]
    for d in range(1, NY):
        tile = tile + br[10 + d]
    bg[...] = tile
    for cp in back[1] + back[2] + back[3] + [mixed_copy]:
        cp.wait()
    for n, d in enumerate(ORDER):
        ycp[n].wait()
        val = val + yr[d].astype(F32)
    wg[...] = val


def finish_kernel(*refs):
    for src, dst in zip(refs[:6], refs[6:]):
        dst[...] = src[:dst.shape[0], :dst.shape[1]]


VM = pl.BlockSpec(memory_space=pltpu.VMEM)
SM = pl.BlockSpec(memory_space=pltpu.SMEM)
ANY = pl.BlockSpec(memory_space=pl.ANY)
DMA = pltpu.SemaphoreType.DMA
LIMIT = 62 * 1024 * 1024


def sds(shape, dtype):
    return jax.ShapeDtypeStruct(shape, dtype)


def on_device(queries, keys, values, d_mixed, series_ids, variate_ids, variate_bias, w_out):
    tokens = sds((TOK, D), BF16)
    wide = pltpu.VMEM((ROW, 128), BF16)
    wide32 = pltpu.VMEM((ROW, 128), F32)
    pair = pltpu.VMEM((2, ROW, 128), BF16)
    square = pltpu.VMEM((2, ROW, ROW), BF16)
    results = pl.pallas_call(
        fused_kernel,
        out_shape=[tokens] * 4 + [sds((16, D), F32), sds((8, 128), F32)],
        in_specs=[ANY] * 7 + [SM],
        out_specs=[ANY] * 4 + [VM] * 2,
        scratch_shapes=[
            pltpu.VMEM((TOK, D), BF16), pltpu.VMEM((TOK, D), BF16),
            wide, wide, wide, wide,
            pltpu.VMEM((1, ROW), jnp.int32), pltpu.VMEM((1, ROW), jnp.int32),
            pltpu.VMEM((NX, NZ, NC, 16, D), BF16), pltpu.VMEM((TOK, D), BF16),
            wide32, pair, pair, pair, pltpu.VMEM((128, ROW), BF16),
            square, square, wide32, wide32, wide, pltpu.VMEM((128, ROW), BF16),
            pltpu.VMEM((128, 256), F32), pltpu.VMEM((128, 256), F32),
            wide, wide, wide, wide,
            pltpu.VMEM((TOK, D), BF16),
            pltpu.VMEM((NX, NZ, NC, 16, D), BF16), pltpu.VMEM((NX, NZ, 16, D), BF16),
            pltpu.VMEM((8, NX, 16, D), BF16), pltpu.VMEM((8, NX, 16, D), F32), pltpu.VMEM((8, NX, 16, D), BF16),
            pltpu.VMEM((8, 16, D), BF16), pltpu.VMEM((8, 16, D), BF16),
            pltpu.VMEM((16, D), BF16), pltpu.VMEM((8, 16, D), BF16),
            pltpu.VMEM((4, 8, 128), F32), pltpu.VMEM((18, 8, 128), F32),
            DMA((8, 8)), DMA((8, 8)), DMA((8,)),
            DMA((2, 8)), DMA((2, 8)), DMA((2,)),
            DMA((8,)), DMA((8,)),
            DMA((8, 4)), DMA((8, 4)),
            DMA((8,)), DMA((8,)), DMA((2,)),
            DMA((8,)), DMA((8,)),
            DMA((8, 4)), DMA((8, 4)),
            DMA((8,)), DMA((8,)),
            DMA((8,)), DMA((8,)),
            DMA((18,)), DMA((18,)),
        ],
        compiler_params=pltpu.CompilerParams(collective_id=0, has_side_effects=True, vmem_limit_bytes=LIMIT),
        name="fused",
    )(queries[0], keys[0], values[0], d_mixed[0], series_ids, variate_ids, w_out, variate_bias)
    mixed, dq, dk, dv, wg, bg = pl.pallas_call(
        finish_kernel,
        out_shape=[tokens] * 4 + [sds((16, D), F32), sds((2, HEADS), F32)],
        in_specs=[VM] * 6,
        out_specs=[VM] * 6,
        compiler_params=pltpu.CompilerParams(vmem_limit_bytes=LIMIT),
        name="finish",
    )(*results)
    return mixed[None], dq[None], dk[None], dv[None], wg, bg


def solution(mesh):
    finer = Mesh(mesh.devices.reshape(NY, NX, NZ, NC), ("ctx", "x", "z", "core"))
    tokens = P(DP, "ctx", None)
    ids = P(DP, "ctx")
    return jax.shard_map(
        on_device,
        mesh=finer,
        in_specs=(tokens, tokens, tokens, tokens, ids, ids, P(), P(DP, None)),
        out_specs=(tokens, tokens, tokens, tokens, P(DP, None), P()),
        check_vma=False,
    )
```

```python
import functools

import jax
import jax.numpy as jnp
from jax import lax
from jax.experimental import pallas as pl
from jax.experimental.pallas import tpu as pltpu
from jax.sharding import Mesh
from jax.sharding import PartitionSpec as P

HEADS = 16
HEAD_DIM = 64
NY, NX, NZ, NC = 8, 4, 8, 2
TOK = 128
ROW = 1024
D = 1024
DP = ("x", "z", "core")
MESH = pl.DeviceIdType.MESH
F32 = jnp.float32
BF16 = jnp.bfloat16
ORDER = (1, 7, 2, 6, 3, 5, 4)
LATE = (4, 5, 3, 6, 2, 7, 1, 0)
MASK = 2048.0
BQ = 256


def remote(src, dst, ssem, rsem, **where):
    return pltpu.make_async_remote_copy(
        src_ref=src, dst_ref=dst, send_sem=ssem, recv_sem=rsem,
        device_id=where, device_id_type=MESH,
    )


def meet(peers):
    sem = pltpu.get_barrier_semaphore()
    for peer in peers:
        pl.semaphore_signal(sem, inc=1, device_id=peer, device_id_type=MESH)
    pl.semaphore_wait(sem, len(peers))


def others(axis, n):
    me = lax.axis_index(axis)
    return [{axis: lax.rem(me + d, n)} for d in range(1, n)]


def span(i, n=128):
    return pl.ds(pl.multiple_of(i * n, n), n)


def spread(src, dst, ssem, rsem, lsem):
    me = lax.axis_index("ctx")
    copies = []
    for d in ORDER:
        to = lax.rem(me + d, NY)
        c = remote(src.at[:, span(to)], dst.at[span(me), :], ssem.at[d], rsem.at[d], ctx=to)
        c.start()
        copies.append(c)
    c = pltpu.make_async_copy(src.at[:, span(me)], dst.at[span(me), :], lsem)
    c.start()
    copies.append(c)
    return copies


def unspread(src, dst, ssem, rsem, lsem):
    me = lax.axis_index("ctx")
    copies = []
    for d in ORDER:
        to = lax.rem(me + d, NY)
        c = remote(src.at[span(to), :], dst.at[:, span(me)], ssem.at[d], rsem.at[d], ctx=to)
        c.start()
        copies.append(c)
    c = pltpu.make_async_copy(src.at[span(me), :], dst.at[:, span(me)], lsem)
    c.start()
    copies.append(c)
    return copies


def fused_kernel(q, k, v, dm_in, ser, var, w, bias,
                 mixed_o, dq, dk, dv, wg, bg,
                 dm, mixed, qh, kh, vh, dh, ser_o, var_o, wf, dctx,
                 base_s, qa_s, ka_s, va_s, qt_s, eb_s, ds_s, c_s32, inv_s, dn_s, dnt_s, dkt, dvt,
                 ctxh, dqh, dkh, dvh,
                 ctx, g, sa, hs, hf, hr, zs, zr, ys, yr, bs, br,
                 a_s, a_r, a_l, i_s, i_r, i_l, wz_s, wz_r, wx_s, wx_r, wc_s, wc_r, w_l,
                 c_s, c_r, x_s, x_r, z_s, z_r, y_s, y_r, b_s, b_r):
    y, x, z, c = (lax.axis_index(a) for a in ("ctx", "x", "z", "core"))
    sib = 1 - c
    dm_copy = pltpu.make_async_copy(dm_in, dm, w_l.at[1])
    dm_copy.start()
    own = pltpu.make_async_copy(w, wf.at[x, z, c], w_l.at[0])
    own.start()
    meet(others("ctx", NY) + others("x", NX) + others("z", NZ) + [{"core": sib}])

    from_z, from_x = {}, {}
    for d in ORDER:
        cp = remote(w, wf.at[x, z, c], wz_s.at[d], wz_r.at[d], z=lax.rem(z + d, NZ))
        cp.start()
        from_z[d] = cp

    def to_x(e):
        src = wf.at[x, lax.rem(z + NZ - e, NZ), c]
        for d in range(1, NX):
            cp = remote(w if e == 0 else src, src, wx_s.at[e, d], wx_r.at[e, d], x=lax.rem(x + d, NX))
            cp.start()
            from_x[e, d] = cp

    to_x(0)
    ids, ins = [], []

    def send_ids():
        for n, (src, dst) in enumerate(((ser, ser_o), (var, var_o))):
            for d in ORDER:
                cp = remote(src, dst.at[:, span(y)], i_s.at[n, d], i_r.at[n, d], ctx=lax.rem(y + d, NY))
                cp.start()
                ids.append(cp)
            cp = pltpu.make_async_copy(src, dst.at[:, span(y)], i_l.at[n])
            cp.start()
            ids.append(cp)

    for n, (src, dst) in enumerate(((q, qh), (k, kh), (v, vh))):
        if n == 2:
            send_ids()
        ins.append(spread(src, dst, a_s.at[n], a_r.at[n], a_l.at[n]))

    own.wait()
    siblings = []

    def to_sibling(e):
        for d in range(1, NX):
            from_x[e, d].wait()
        part = wf.at[:, lax.rem(z + NZ - e, NZ), c]
        cp = remote(part, part, wc_s.at[e], wc_r.at[e], core=sib)
        cp.start()
        siblings.append(cp)

    for e in ORDER:
        from_z[e].wait()
        to_x(e)

    for cp in ids + ins[0] + ins[1]:
        cp.wait()
    feat = lax.broadcasted_iota(jnp.int32, (128, ROW), 0) % 64
    held = jnp.where(feat < 16, ser_o[...], var_o[...])
    want = jnp.where(feat < 16, feat, jnp.where(feat < 28, feat % 4, -1))
    base = jnp.where(held == want, 1.0, 0.0).T
    base_s[...] = base
    lane = lax.broadcasted_iota(jnp.int32, (1, 128), 1)
    within = lane % 64
    half = [slice(0, 64), slice(64, 128)]
    mine = [lane < 64, lane >= 64]
    qt_s[...] = (qh[...].astype(F32) * 0.125).T.astype(BF16)
    for h in range(2):
        gap = jnp.full((1, 128), bias[0, 2 * y + h] - bias[1, 2 * y + h], F32)
        hi = gap.astype(BF16).astype(F32)
        mid = (gap - hi).astype(BF16).astype(F32)
        low = gap - hi - mid
        coef = jnp.where(within < 16, MASK, jnp.where(within < 20, hi, jnp.where(within < 24, mid, low)))
        qa_s[h] = jnp.where(mine[h], qh[...].astype(F32) * 0.125, base * coef).astype(BF16)
        ka_s[h] = jnp.where(mine[h], kh[...].astype(F32), base).astype(BF16)
    def scores(i, carry):
        rows = span(i, BQ)
        for h in range(2):
            s = lax.dot_general(qa_s[h, rows, :], ka_s[h], (((1,), (1,)), ((), ())),
                                preferred_element_type=F32)
            top = jnp.max(s, axis=1, keepdims=True)
            eb_s[h, rows, :] = jnp.exp(s - top).astype(BF16)
        return carry

    lax.fori_loop(0, ROW // BQ, scores, 0)
    for e in (0,) + ORDER:
        to_sibling(e)
    for cp in ins[2]:
        cp.wait()
    for h in range(2):
        va_s[h] = jnp.where(mine[h], vh[...].astype(F32), 1.0).astype(BF16)

    def forward(i, carry):
        rows = span(i, BQ)
        un = [jnp.dot(eb_s[h, rows, :], va_s[h], preferred_element_type=F32) for h in range(2)]
        inv = 1.0 / pltpu.roll(jnp.where(mine[0], un[1], un[0]), 64, 1)
        mix = jnp.where(mine[0], un[0], un[1]) * inv
        inv_s[rows, :] = inv
        c_s32[rows, :] = mix
        ctxh[rows, :] = mix.astype(BF16)
        return carry

    lax.fori_loop(0, ROW // BQ, forward, 0)
    back = [unspread(ctxh, ctx, a_s.at[4], a_r.at[4], a_l.at[4])]

    for cp in siblings:
        cp.wait()
    dm_copy.wait()
    for xi in range(NX):
        rows = wf[xi].reshape(256, D)
        got = lax.dot_general(dm[...], rows, (((1,), (1,)), ((), ())), preferred_element_type=F32)
        dctx[:, 256 * xi:256 * (xi + 1)] = got.astype(BF16)
    ins.append(spread(dctx, dh, a_s.at[3], a_r.at[3], a_l.at[3]))

    for cp in back[0]:
        cp.wait()
    for xi in range(NX):
        part = ctx[:, 256 * xi:256 * (xi + 1)].astype(F32).T.astype(BF16)
        got = jnp.dot(part, dm[...], preferred_element_type=F32)
        g[xi] = got.astype(BF16).reshape(8, 2, 16, D)
    sibs = {}
    for off in LATE:
        zt = lax.rem(z + off, NZ)
        cp = remote(g.at[:, zt, sib], sa.at[:, zt], c_s.at[off], c_r.at[off], core=sib)
        cp.start()
        sibs[off] = cp

    xcp, zcp = {}, []

    def sum_cores(off):
        zt = lax.rem(z + off, NZ)
        sibs[off].wait()
        val = g[:, zt, c].astype(F32) + sa[:, zt].astype(F32)
        hf[off] = val
        hs[off] = val.astype(BF16)
        for d in range(1, NX):
            to = lax.rem(x + d, NX)
            cp = remote(hs.at[off, to], hr.at[off, d], x_s.at[off, d], x_r.at[off, d], x=to)
            cp.start()
            xcp[off, d] = cp

    ins[3][-1].wait()

    def queries_grad(n, carry):
        pair = []
        for m in range(2):
            at = 2 * n + m
            odd = at % 2
            d = odd * ((at + 1) // 2) + (1 - odd) * ((NY - at // 2) % NY)
            to = lax.rem(y + d, NY)
            cp = remote(dctx.at[:, span(to)], dh.at[span(y), :], a_s.at[3, d], a_r.at[3, d], ctx=to)
            if m:
                cp.wait()
            else:
                pl.when(n > 0)(cp.wait)
            pair.append(span(lax.rem(y + NY - d, NY)))

        def both(ref, *lead):
            return jnp.concatenate([ref[(*lead, r, slice(None))] for r in pair], axis=0)

        def keep(ref, val, *lead):
            for m in range(2):
                ref[(*lead, pair[m], slice(None))] = val[128 * m:128 * (m + 1)]

        dn = (both(dh).astype(F32) * both(inv_s)).astype(BF16)
        keep(dn_s, dn)
        dnf = dn.astype(F32)
        prod = dnf * both(c_s32)
        o_blk = both(base_s)
        outs, sums = [], []
        for h in range(2):
            delta = jnp.sum(jnp.where(mine[h], prod, 0.0), axis=1, keepdims=True)
            hi = delta.astype(BF16).astype(F32)
            mid = (delta - hi).astype(BF16).astype(F32)
            low = delta - hi - mid
            da = jnp.where(within == 0, -hi, jnp.where(within == 1, -mid, jnp.where(within == 2, -low, 0.0)))
            da = jnp.where(mine[h], dnf, da).astype(BF16)
            t = lax.dot_general(da, va_s[h], (((1,), (1,)), ((), ())), preferred_element_type=F32)
            ds = (both(eb_s, h).astype(F32) * t).astype(BF16)
            keep(ds_s, ds, h)
            got = jnp.dot(ds, ka_s[h], preferred_element_type=F32)
            u = jnp.where(mine[1 - h] & (within >= 16) & (within < 20), got, 0.0)
            sums.append(jnp.sum(u * o_blk, axis=0, keepdims=True))
            sums.append(jnp.sum(u * (1.0 - o_blk), axis=0, keepdims=True))
            outs.append(got)
        keep(dqh, (jnp.where(mine[0], outs[0], outs[1]) * 0.125).astype(BF16))
        return tuple(a + b for a, b in zip(carry, sums))

    zero = jnp.zeros((1, 128), F32)
    sums = lax.fori_loop(0, 4, queries_grad, (zero,) * 4)
    back.append(unspread(dqh, dq, a_s.at[6], a_r.at[6], a_l.at[6]))
    for off in LATE:
        sum_cores(off)
    dnt_s[...] = dn_s[...].astype(F32).T.astype(BF16)

    def values_grad(j, carry):
        cols = span(j, 256)
        for h in range(2):
            dvt[half[h], :] = jnp.dot(dnt_s[half[h], :], eb_s[h, :, cols], preferred_element_type=F32)
        dvh[cols, :] = dvt[...].T.astype(BF16)
        return carry

    lax.fori_loop(0, ROW // 256, values_grad, 0)
    back.append(unspread(dvh, dv, a_s.at[5], a_r.at[5], a_l.at[5]))
    total = [jnp.sum(a, axis=1, keepdims=True) for a in sums]
    row = lax.broadcasted_iota(jnp.int32, (8, 128), 0)
    col = lax.broadcasted_iota(jnp.int32, (8, 128), 1) - 2 * y
    tile = jnp.zeros((8, 128), F32)
    for h in range(2):
        for r in range(2):
            tile = jnp.where((row == r) & (col == h), total[2 * h + r], tile)
    bs[3] = tile
    bsib = remote(bs.at[3], br.at[0], b_s.at[0], b_r.at[0], core=sib)
    bsib.start()

    def keys_grad(j, carry):
        cols = span(j, 256)
        for h in range(2):
            dkt[half[h], :] = jnp.dot(qt_s[half[h], :], ds_s[h, :, cols], preferred_element_type=F32)
        dkh[cols, :] = dkt[...].T.astype(BF16)
        return carry

    lax.fori_loop(0, ROW // 256, keys_grad, 0)
    back.append(unspread(dkh, dk, a_s.at[7], a_r.at[7], a_l.at[7]))

    for n in range(4):
        cols = slice(256 * n, 256 * (n + 1))
        got = jnp.dot(ctx[...], wf[...].reshape(D, D)[:, cols], preferred_element_type=F32)
        mixed[:, cols] = got.astype(BF16)
    mixed_copy = pltpu.make_async_copy(mixed, mixed_o, w_l.at[0])
    mixed_copy.start()
    bsib.wait()
    bs[0] = bs[3] + br[0]
    bz = []
    for d in range(1, NZ):
        cp = remote(bs.at[0], br.at[d], b_s.at[d], b_r.at[d], z=lax.rem(z + d, NZ))
        cp.start()
        bz.append(cp)

    for off in LATE:
        for d in range(1, NX):
            xcp[off, d].wait()
        val = hf[off, x] + hr[off, 1].astype(F32) + hr[off, 2].astype(F32) + hr[off, 3].astype(F32)
        if off:
            zs[off] = val.astype(BF16)
            cp = remote(zs.at[off], zr.at[off], z_s.at[off], z_r.at[off], z=lax.rem(z + off, NZ))
            cp.start()
            zcp.append(cp)
        if off == 4:
            for cp in bz:
                cp.wait()
            tile = bs[0]
            for d in range(1, NZ):
                tile = tile + br[d]
            bs[1] = tile
            bx = []
            for d in range(1, NX):
                cp = remote(bs.at[1], br.at[7 + d], b_s.at[7 + d], b_r.at[7 + d], x=lax.rem(x + d, NX))
                cp.start()
                bx.append(cp)
    for cp in bx:
        cp.wait()
    bs[2] = bs[1] + br[8] + br[9] + br[10]
    by = []
    for d in range(1, NY):
        cp = remote(bs.at[2], br.at[10 + d], b_s.at[10 + d], b_r.at[10 + d], ctx=lax.rem(y + d, NY))
        cp.start()
        by.append(cp)
    for cp in zcp:
        cp.wait()
    for d in range(1, NZ):
        val = val + zr[d].astype(F32)
    ys[...] = val.astype(BF16)
    ycp = []
    for d in ORDER:
        cp = remote(ys, yr.at[d], y_s.at[d], y_r.at[d], ctx=lax.rem(y + d, NY))
        cp.start()
        ycp.append(cp)
    for cp in by:
        cp.wait()
    tile = bs[2]
    for d in range(1, NY):
        tile = tile + br[10 + d]
    bg[...] = tile
    for cp in back[1] + back[2] + back[3] + [mixed_copy]:
        cp.wait()
    for n, d in enumerate(ORDER):
        ycp[n].wait()
        val = val + yr[d].astype(F32)
    wg[...] = val


def finish_kernel(*refs):
    for src, dst in zip(refs[:6], refs[6:]):
        dst[...] = src[:dst.shape[0], :dst.shape[1]]


VM = pl.BlockSpec(memory_space=pltpu.VMEM)
SM = pl.BlockSpec(memory_space=pltpu.SMEM)
ANY = pl.BlockSpec(memory_space=pl.ANY)
DMA = pltpu.SemaphoreType.DMA
LIMIT = 62 * 1024 * 1024


def sds(shape, dtype):
    return jax.ShapeDtypeStruct(shape, dtype)


def on_device(queries, keys, values, d_mixed, series_ids, variate_ids, variate_bias, w_out):
    tokens = sds((TOK, D), BF16)
    wide = pltpu.VMEM((ROW, 128), BF16)
    wide32 = pltpu.VMEM((ROW, 128), F32)
    pair = pltpu.VMEM((2, ROW, 128), BF16)
    square = pltpu.VMEM((2, ROW, ROW), BF16)
    results = pl.pallas_call(
        fused_kernel,
        out_shape=[tokens] * 4 + [sds((16, D), F32), sds((8, 128), F32)],
        in_specs=[ANY] * 7 + [SM],
        out_specs=[ANY] * 4 + [VM] * 2,
        scratch_shapes=[
            pltpu.VMEM((TOK, D), BF16), pltpu.VMEM((TOK, D), BF16),
            wide, wide, wide, wide,
            pltpu.VMEM((1, ROW), jnp.int32), pltpu.VMEM((1, ROW), jnp.int32),
            pltpu.VMEM((NX, NZ, NC, 16, D), BF16), pltpu.VMEM((TOK, D), BF16),
            wide32, pair, pair, pair, pltpu.VMEM((128, ROW), BF16),
            square, square, wide32, wide32, wide, pltpu.VMEM((128, ROW), BF16),
            pltpu.VMEM((128, 256), F32), pltpu.VMEM((128, 256), F32),
            wide, wide, wide, wide,
            pltpu.VMEM((TOK, D), BF16),
            pltpu.VMEM((NX, NZ, NC, 16, D), BF16), pltpu.VMEM((NX, NZ, 16, D), BF16),
            pltpu.VMEM((8, NX, 16, D), BF16), pltpu.VMEM((8, NX, 16, D), F32), pltpu.VMEM((8, NX, 16, D), BF16),
            pltpu.VMEM((8, 16, D), BF16), pltpu.VMEM((8, 16, D), BF16),
            pltpu.VMEM((16, D), BF16), pltpu.VMEM((8, 16, D), BF16),
            pltpu.VMEM((4, 8, 128), F32), pltpu.VMEM((18, 8, 128), F32),
            DMA((8, 8)), DMA((8, 8)), DMA((8,)),
            DMA((2, 8)), DMA((2, 8)), DMA((2,)),
            DMA((8,)), DMA((8,)),
            DMA((8, 4)), DMA((8, 4)),
            DMA((8,)), DMA((8,)), DMA((2,)),
            DMA((8,)), DMA((8,)),
            DMA((8, 4)), DMA((8, 4)),
            DMA((8,)), DMA((8,)),
            DMA((8,)), DMA((8,)),
            DMA((18,)), DMA((18,)),
        ],
        compiler_params=pltpu.CompilerParams(collective_id=0, has_side_effects=True, vmem_limit_bytes=LIMIT),
        name="fused",
    )(queries[0], keys[0], values[0], d_mixed[0], series_ids, variate_ids, w_out, variate_bias)
    mixed, dq, dk, dv, wg, bg = pl.pallas_call(
        finish_kernel,
        out_shape=[tokens] * 4 + [sds((16, D), F32), sds((2, HEADS), F32)],
        in_specs=[VM] * 6,
        out_specs=[VM] * 6,
        compiler_params=pltpu.CompilerParams(vmem_limit_bytes=LIMIT),
        name="finish",
    )(*results)
    return mixed[None], dq[None], dk[None], dv[None], wg, bg


def solution(mesh):
    finer = Mesh(mesh.devices.reshape(NY, NX, NZ, NC), ("ctx", "x", "z", "core"))
    tokens = P(DP, "ctx", None)
    ids = P(DP, "ctx")
    return jax.shard_map(
        on_device,
        mesh=finer,
        in_specs=(tokens, tokens, tokens, tokens, ids, ids, P(), P(DP, None)),
        out_specs=(tokens, tokens, tokens, tokens, P(DP, None), P()),
        check_vma=False,
    )
```

```python
import functools

import jax
import jax.numpy as jnp
from jax import lax
from jax.experimental import pallas as pl
from jax.experimental.pallas import tpu as pltpu
from jax.sharding import Mesh
from jax.sharding import PartitionSpec as P

HEADS = 16
HEAD_DIM = 64
NY, NX, NZ, NC = 8, 4, 8, 2
TOK = 128
ROW = 1024
D = 1024
DP = ("x", "z", "core")
MESH = pl.DeviceIdType.MESH
F32 = jnp.float32
BF16 = jnp.bfloat16
ORDER = (1, 7, 2, 6, 3, 5, 4)
LATE = (4, 5, 3, 6, 2, 7, 1, 0)
MASK = 2048.0
BQ = 256


def remote(src, dst, ssem, rsem, **where):
    return pltpu.make_async_remote_copy(
        src_ref=src, dst_ref=dst, send_sem=ssem, recv_sem=rsem,
        device_id=where, device_id_type=MESH,
    )


def meet(peers):
    sem = pltpu.get_barrier_semaphore()
    for peer in peers:
        pl.semaphore_signal(sem, inc=1, device_id=peer, device_id_type=MESH)
    pl.semaphore_wait(sem, len(peers))


def others(axis, n):
    me = lax.axis_index(axis)
    return [{axis: lax.rem(me + d, n)} for d in range(1, n)]


def span(i, n=128):
    return pl.ds(pl.multiple_of(i * n, n), n)


def spread(src, dst, ssem, rsem, lsem):
    me = lax.axis_index("ctx")
    copies = []
    for d in ORDER:
        to = lax.rem(me + d, NY)
        c = remote(src.at[:, span(to)], dst.at[span(me), :], ssem.at[d], rsem.at[d], ctx=to)
        c.start()
        copies.append(c)
    c = pltpu.make_async_copy(src.at[:, span(me)], dst.at[span(me), :], lsem)
    c.start()
    copies.append(c)
    return copies


def unspread(src, dst, ssem, rsem, lsem):
    me = lax.axis_index("ctx")
    copies = []
    for d in ORDER:
        to = lax.rem(me + d, NY)
        c = remote(src.at[span(to), :], dst.at[:, span(me)], ssem.at[d], rsem.at[d], ctx=to)
        c.start()
        copies.append(c)
    c = pltpu.make_async_copy(src.at[span(me), :], dst.at[:, span(me)], lsem)
    c.start()
    copies.append(c)
    return copies


def fused_kernel(q, k, v, dm_in, ser, var, w, bias,
                 mixed_o, dq, dk, dv, wg, bg,
                 dm, mixed, qh, kh, vh, dh, ser_o, var_o, wf, dctx,
                 base_s, qa_s, ka_s, va_s, qt_s, eb_s, ds_s, c_s32, inv_s, dn_s, dnt_s, dkt, dvt,
                 ctxh, dqh, dkh, dvh,
                 ctx, g, sa, hs, hf, hr, zs, zr, ys, yr, bs, br,
                 a_s, a_r, a_l, i_s, i_r, i_l, wz_s, wz_r, wx_s, wx_r, wc_s, wc_r, w_l,
                 c_s, c_r, x_s, x_r, z_s, z_r, y_s, y_r, b_s, b_r):
    y, x, z, c = (lax.axis_index(a) for a in ("ctx", "x", "z", "core"))
    sib = 1 - c
    dm_copy = pltpu.make_async_copy(dm_in, dm, w_l.at[1])
    dm_copy.start()
    own = pltpu.make_async_copy(w, wf.at[x, z, c], w_l.at[0])
    own.start()
    meet(others("ctx", NY) + others("x", NX) + others("z", NZ) + [{"core": sib}])

    ins = [spread(q, qh, a_s.at[0], a_r.at[0], a_l.at[0])]
    from_z, from_x = {}, {}
    for d in ORDER:
        cp = remote(w, wf.at[x, z, c], wz_s.at[d], wz_r.at[d], z=lax.rem(z + d, NZ))
        cp.start()
        from_z[d] = cp

    def to_x(e):
        src = wf.at[x, lax.rem(z + NZ - e, NZ), c]
        for d in range(1, NX):
            cp = remote(w if e == 0 else src, src, wx_s.at[e, d], wx_r.at[e, d], x=lax.rem(x + d, NX))
            cp.start()
            from_x[e, d] = cp

    to_x(0)
    ids = []

    def send_ids():
        for n, (src, dst) in enumerate(((ser, ser_o), (var, var_o))):
            for d in ORDER:
                cp = remote(src, dst.at[:, span(y)], i_s.at[n, d], i_r.at[n, d], ctx=lax.rem(y + d, NY))
                cp.start()
                ids.append(cp)
            cp = pltpu.make_async_copy(src, dst.at[:, span(y)], i_l.at[n])
            cp.start()
            ids.append(cp)

    for n, (src, dst) in ((1, (k, kh)), (2, (v, vh))):
        if n == 2:
            send_ids()
        ins.append(spread(src, dst, a_s.at[n], a_r.at[n], a_l.at[n]))

    own.wait()
    siblings = []

    def to_sibling(e):
        for d in range(1, NX):
            from_x[e, d].wait()
        part = wf.at[:, lax.rem(z + NZ - e, NZ), c]
        cp = remote(part, part, wc_s.at[e], wc_r.at[e], core=sib)
        cp.start()
        siblings.append(cp)

    for e in ORDER:
        from_z[e].wait()
        to_x(e)

    for cp in ids + ins[0] + ins[1]:
        cp.wait()
    feat = lax.broadcasted_iota(jnp.int32, (128, ROW), 0) % 64
    held = jnp.where(feat < 16, ser_o[...], var_o[...])
    want = jnp.where(feat < 16, feat, jnp.where(feat < 28, feat % 4, -1))
    base = jnp.where(held == want, 1.0, 0.0).T
    base_s[...] = base
    lane = lax.broadcasted_iota(jnp.int32, (1, 128), 1)
    within = lane % 64
    half = [slice(0, 64), slice(64, 128)]
    mine = [lane < 64, lane >= 64]
    qt_s[...] = (qh[...].astype(F32) * 0.125).T.astype(BF16)
    for h in range(2):
        gap = jnp.full((1, 128), bias[0, 2 * y + h] - bias[1, 2 * y + h], F32)
        hi = gap.astype(BF16).astype(F32)
        mid = (gap - hi).astype(BF16).astype(F32)
        low = gap - hi - mid
        coef = jnp.where(within < 16, MASK, jnp.where(within < 20, hi, jnp.where(within < 24, mid, low)))
        qa_s[h] = jnp.where(mine[h], qh[...].astype(F32) * 0.125, base * coef).astype(BF16)
        ka_s[h] = jnp.where(mine[h], kh[...].astype(F32), base).astype(BF16)
    def scores(i, carry):
        rows = span(i, BQ)
        for h in range(2):
            s = lax.dot_general(qa_s[h, rows, :], ka_s[h], (((1,), (1,)), ((), ())),
                                preferred_element_type=F32)
            top = jnp.max(s, axis=1, keepdims=True)
            eb_s[h, rows, :] = jnp.exp(s - top).astype(BF16)
        return carry

    lax.fori_loop(0, ROW // BQ, scores, 0)
    for e in (0,) + ORDER:
        to_sibling(e)
    for cp in ins[2]:
        cp.wait()
    for h in range(2):
        va_s[h] = jnp.where(mine[h], vh[...].astype(F32), 1.0).astype(BF16)

    def forward(i, carry):
        rows = span(i, BQ)
        un = [jnp.dot(eb_s[h, rows, :], va_s[h], preferred_element_type=F32) for h in range(2)]
        inv = 1.0 / pltpu.roll(jnp.where(mine[0], un[1], un[0]), 64, 1)
        mix = jnp.where(mine[0], un[0], un[1]) * inv
        inv_s[rows, :] = inv
        c_s32[rows, :] = mix
        ctxh[rows, :] = mix.astype(BF16)
        return carry

    lax.fori_loop(0, ROW // BQ, forward, 0)
    back = [unspread(ctxh, ctx, a_s.at[4], a_r.at[4], a_l.at[4])]

    for cp in siblings:
        cp.wait()
    dm_copy.wait()
    for xi in range(NX):
        rows = wf[xi].reshape(256, D)
        got = lax.dot_general(dm[...], rows, (((1,), (1,)), ((), ())), preferred_element_type=F32)
        dctx[:, 256 * xi:256 * (xi + 1)] = got.astype(BF16)
    ins.append(spread(dctx, dh, a_s.at[3], a_r.at[3], a_l.at[3]))

    for cp in back[0]:
        cp.wait()
    for xi in range(NX):
        part = ctx[:, 256 * xi:256 * (xi + 1)].astype(F32).T.astype(BF16)
        got = jnp.dot(part, dm[...], preferred_element_type=F32)
        g[xi] = got.astype(BF16).reshape(8, 2, 16, D)
    sibs = {}
    for off in LATE:
        zt = lax.rem(z + off, NZ)
        cp = remote(g.at[:, zt, sib], sa.at[:, zt], c_s.at[off], c_r.at[off], core=sib)
        cp.start()
        sibs[off] = cp

    xcp, zcp = {}, []

    def sum_cores(off):
        zt = lax.rem(z + off, NZ)
        sibs[off].wait()
        val = g[:, zt, c].astype(F32) + sa[:, zt].astype(F32)
        hf[off] = val
        hs[off] = val.astype(BF16)
        for d in range(1, NX):
            to = lax.rem(x + d, NX)
            cp = remote(hs.at[off, to], hr.at[off, d], x_s.at[off, d], x_r.at[off, d], x=to)
            cp.start()
            xcp[off, d] = cp

    ins[3][-1].wait()

    def queries_grad(n, carry):
        pair = []
        for m in range(2):
            at = 2 * n + m
            odd = at % 2
            d = odd * ((at + 1) // 2) + (1 - odd) * ((NY - at // 2) % NY)
            to = lax.rem(y + d, NY)
            cp = remote(dctx.at[:, span(to)], dh.at[span(y), :], a_s.at[3, d], a_r.at[3, d], ctx=to)
            if m:
                cp.wait()
            else:
                pl.when(n > 0)(cp.wait)
            pair.append(span(lax.rem(y + NY - d, NY)))

        def both(ref, *lead):
            return jnp.concatenate([ref[(*lead, r, slice(None))] for r in pair], axis=0)

        def keep(ref, val, *lead):
            for m in range(2):
                ref[(*lead, pair[m], slice(None))] = val[128 * m:128 * (m + 1)]

        dn = (both(dh).astype(F32) * both(inv_s)).astype(BF16)
        keep(dn_s, dn)
        dnf = dn.astype(F32)
        prod = dnf * both(c_s32)
        o_blk = both(base_s)
        outs, sums = [], []
        for h in range(2):
            delta = jnp.sum(jnp.where(mine[h], prod, 0.0), axis=1, keepdims=True)
            hi = delta.astype(BF16).astype(F32)
            mid = (delta - hi).astype(BF16).astype(F32)
            low = delta - hi - mid
            da = jnp.where(within == 0, -hi, jnp.where(within == 1, -mid, jnp.where(within == 2, -low, 0.0)))
            da = jnp.where(mine[h], dnf, da).astype(BF16)
            t = lax.dot_general(da, va_s[h], (((1,), (1,)), ((), ())), preferred_element_type=F32)
            ds = (both(eb_s, h).astype(F32) * t).astype(BF16)
            keep(ds_s, ds, h)
            got = jnp.dot(ds, ka_s[h], preferred_element_type=F32)
            u = jnp.where(mine[1 - h] & (within >= 16) & (within < 20), got, 0.0)
            sums.append(jnp.sum(u * o_blk, axis=0, keepdims=True))
            sums.append(jnp.sum(u * (1.0 - o_blk), axis=0, keepdims=True))
            outs.append(got)
        keep(dqh, (jnp.where(mine[0], outs[0], outs[1]) * 0.125).astype(BF16))
        return tuple(a + b for a, b in zip(carry, sums))

    zero = jnp.zeros((1, 128), F32)
    sums = lax.fori_loop(0, 4, queries_grad, (zero,) * 4)
    back.append(unspread(dqh, dq, a_s.at[6], a_r.at[6], a_l.at[6]))
    for off in LATE:
        sum_cores(off)
    dnt_s[...] = dn_s[...].astype(F32).T.astype(BF16)

    def values_grad(j, carry):
        cols = span(j, 256)
        for h in range(2):
            dvt[half[h], :] = jnp.dot(dnt_s[half[h], :], eb_s[h, :, cols], preferred_element_type=F32)
        dvh[cols, :] = dvt[...].T.astype(BF16)
        return carry

    lax.fori_loop(0, ROW // 256, values_grad, 0)
    back.append(unspread(dvh, dv, a_s.at[5], a_r.at[5], a_l.at[5]))
    total = [jnp.sum(a, axis=1, keepdims=True) for a in sums]
    row = lax.broadcasted_iota(jnp.int32, (8, 128), 0)
    col = lax.broadcasted_iota(jnp.int32, (8, 128), 1) - 2 * y
    tile = jnp.zeros((8, 128), F32)
    for h in range(2):
        for r in range(2):
            tile = jnp.where((row == r) & (col == h), total[2 * h + r], tile)
    bs[3] = tile
    bsib = remote(bs.at[3], br.at[0], b_s.at[0], b_r.at[0], core=sib)
    bsib.start()

    def keys_grad(j, carry):
        cols = span(j, 256)
        for h in range(2):
            dkt[half[h], :] = jnp.dot(qt_s[half[h], :], ds_s[h, :, cols], preferred_element_type=F32)
        dkh[cols, :] = dkt[...].T.astype(BF16)
        return carry

    lax.fori_loop(0, ROW // 256, keys_grad, 0)
    back.append(unspread(dkh, dk, a_s.at[7], a_r.at[7], a_l.at[7]))

    for n in range(4):
        cols = slice(256 * n, 256 * (n + 1))
        got = jnp.dot(ctx[...], wf[...].reshape(D, D)[:, cols], preferred_element_type=F32)
        mixed[:, cols] = got.astype(BF16)
    mixed_copy = pltpu.make_async_copy(mixed, mixed_o, w_l.at[0])
    mixed_copy.start()
    bsib.wait()
    bs[0] = bs[3] + br[0]
    bz = []
    for d in range(1, NZ):
        cp = remote(bs.at[0], br.at[d], b_s.at[d], b_r.at[d], z=lax.rem(z + d, NZ))
        cp.start()
        bz.append(cp)

    for off in LATE:
        for d in range(1, NX):
            xcp[off, d].wait()
        val = hf[off, x] + hr[off, 1].astype(F32) + hr[off, 2].astype(F32) + hr[off, 3].astype(F32)
        if off:
            zs[off] = val.astype(BF16)
            cp = remote(zs.at[off], zr.at[off], z_s.at[off], z_r.at[off], z=lax.rem(z + off, NZ))
            cp.start()
            zcp.append(cp)
        if off == 4:
            for cp in bz:
                cp.wait()
            tile = bs[0]
            for d in range(1, NZ):
                tile = tile + br[d]
            bs[1] = tile
            bx = []
            for d in range(1, NX):
                cp = remote(bs.at[1], br.at[7 + d], b_s.at[7 + d], b_r.at[7 + d], x=lax.rem(x + d, NX))
                cp.start()
                bx.append(cp)
    for cp in bx:
        cp.wait()
    bs[2] = bs[1] + br[8] + br[9] + br[10]
    by = []
    for d in range(1, NY):
        cp = remote(bs.at[2], br.at[10 + d], b_s.at[10 + d], b_r.at[10 + d], ctx=lax.rem(y + d, NY))
        cp.start()
        by.append(cp)
    for cp in zcp:
        cp.wait()
    for d in range(1, NZ):
        val = val + zr[d].astype(F32)
    ys[...] = val.astype(BF16)
    ycp = []
    for d in ORDER:
        cp = remote(ys, yr.at[d], y_s.at[d], y_r.at[d], ctx=lax.rem(y + d, NY))
        cp.start()
        ycp.append(cp)
    for cp in by:
        cp.wait()
    tile = bs[2]
    for d in range(1, NY):
        tile = tile + br[10 + d]
    bg[...] = tile
    for cp in back[1] + back[2] + back[3] + [mixed_copy]:
        cp.wait()
    for n, d in enumerate(ORDER):
        ycp[n].wait()
        val = val + yr[d].astype(F32)
    wg[...] = val


def finish_kernel(*refs):
    for src, dst in zip(refs[:6], refs[6:]):
        dst[...] = src[:dst.shape[0], :dst.shape[1]]


VM = pl.BlockSpec(memory_space=pltpu.VMEM)
SM = pl.BlockSpec(memory_space=pltpu.SMEM)
ANY = pl.BlockSpec(memory_space=pl.ANY)
DMA = pltpu.SemaphoreType.DMA
LIMIT = 62 * 1024 * 1024


def sds(shape, dtype):
    return jax.ShapeDtypeStruct(shape, dtype)


def on_device(queries, keys, values, d_mixed, series_ids, variate_ids, variate_bias, w_out):
    tokens = sds((TOK, D), BF16)
    wide = pltpu.VMEM((ROW, 128), BF16)
    wide32 = pltpu.VMEM((ROW, 128), F32)
    pair = pltpu.VMEM((2, ROW, 128), BF16)
    square = pltpu.VMEM((2, ROW, ROW), BF16)
    results = pl.pallas_call(
        fused_kernel,
        out_shape=[tokens] * 4 + [sds((16, D), F32), sds((8, 128), F32)],
        in_specs=[ANY] * 7 + [SM],
        out_specs=[ANY] * 4 + [VM] * 2,
        scratch_shapes=[
            pltpu.VMEM((TOK, D), BF16), pltpu.VMEM((TOK, D), BF16),
            wide, wide, wide, wide,
            pltpu.VMEM((1, ROW), jnp.int32), pltpu.VMEM((1, ROW), jnp.int32),
            pltpu.VMEM((NX, NZ, NC, 16, D), BF16), pltpu.VMEM((TOK, D), BF16),
            wide32, pair, pair, pair, pltpu.VMEM((128, ROW), BF16),
            square, square, wide32, wide32, wide, pltpu.VMEM((128, ROW), BF16),
            pltpu.VMEM((128, 256), F32), pltpu.VMEM((128, 256), F32),
            wide, wide, wide, wide,
            pltpu.VMEM((TOK, D), BF16),
            pltpu.VMEM((NX, NZ, NC, 16, D), BF16), pltpu.VMEM((NX, NZ, 16, D), BF16),
            pltpu.VMEM((8, NX, 16, D), BF16), pltpu.VMEM((8, NX, 16, D), F32), pltpu.VMEM((8, NX, 16, D), BF16),
            pltpu.VMEM((8, 16, D), BF16), pltpu.VMEM((8, 16, D), BF16),
            pltpu.VMEM((16, D), BF16), pltpu.VMEM((8, 16, D), BF16),
            pltpu.VMEM((4, 8, 128), F32), pltpu.VMEM((18, 8, 128), F32),
            DMA((8, 8)), DMA((8, 8)), DMA((8,)),
            DMA((2, 8)), DMA((2, 8)), DMA((2,)),
            DMA((8,)), DMA((8,)),
            DMA((8, 4)), DMA((8, 4)),
            DMA((8,)), DMA((8,)), DMA((2,)),
            DMA((8,)), DMA((8,)),
            DMA((8, 4)), DMA((8, 4)),
            DMA((8,)), DMA((8,)),
            DMA((8,)), DMA((8,)),
            DMA((18,)), DMA((18,)),
        ],
        compiler_params=pltpu.CompilerParams(collective_id=0, has_side_effects=True, vmem_limit_bytes=LIMIT),
        name="fused",
    )(queries[0], keys[0], values[0], d_mixed[0], series_ids, variate_ids, w_out, variate_bias)
    mixed, dq, dk, dv, wg, bg = pl.pallas_call(
        finish_kernel,
        out_shape=[tokens] * 4 + [sds((16, D), F32), sds((2, HEADS), F32)],
        in_specs=[VM] * 6,
        out_specs=[VM] * 6,
        compiler_params=pltpu.CompilerParams(vmem_limit_bytes=LIMIT),
        name="finish",
    )(*results)
    return mixed[None], dq[None], dk[None], dv[None], wg, bg


def solution(mesh):
    finer = Mesh(mesh.devices.reshape(NY, NX, NZ, NC), ("ctx", "x", "z", "core"))
    tokens = P(DP, "ctx", None)
    ids = P(DP, "ctx")
    return jax.shard_map(
        on_device,
        mesh=finer,
        in_specs=(tokens, tokens, tokens, tokens, ids, ids, P(), P(DP, None)),
        out_specs=(tokens, tokens, tokens, tokens, P(DP, None), P()),
        check_vma=False,
    )
```
